512 devices in a mesh: ctx: 64 (over x, z), head: 8 (over y, core).
Axes of the slice: x: 4, y: 4, z: 16, core: 2. Of those that a mesh axis runs over, the one named last changes fastest.
Arguments:
- lin_query: bfloat16 [16384, 4096], P('ctx', 'head'), may hold values from -200 to 200
- lin_keys: bfloat16 [16384, 4096], P('ctx', 'head'), may hold values from -6 to 6
- lin_values: bfloat16 [16384, 4096], P('ctx', 'head'), may hold values from -6 to 6
- lin_grad: bfloat16 [16384, 4096], P('ctx', 'head'), may hold values from -6 to 6
- norm_gain: float32 [4096], P('head'), may hold values from 0.1 to 1.9
- log_decay: float32 [32, 16384], P('head'), may hold values from -1 to 0, as said below
- state_in: bfloat16 [64, 32, 128, 128], P('ctx', 'head'), may hold values from -96 to 96
- soft_query: bfloat16 [16384, 8192], P('ctx', 'head'), may hold values from -10 to 10
- soft_keys: bfloat16 [16384, 1024], P('ctx', 'head'), may hold values from -4 to 4
- soft_values: bfloat16 [16384, 1024], P('ctx', 'head'), may hold values from -6 to 6
- soft_grad: bfloat16 [16384, 8192], P('ctx', 'head'), may hold values from -6 to 6
- projections: bfloat16 [2, 4096, 1024], P(None, None, 'head'), may hold values from -0.125 to 0.125
- doc_lengths: int32 [32], replicated, may hold values from 1 to 768, 16384 in all
Outputs:
- lin_dq: bfloat16 [16384, 4096], P('ctx', 'head')
- lin_dk: bfloat16 [16384, 4096], P('ctx', 'head')
- lin_dv: bfloat16 [16384, 4096], P('ctx', 'head')
- soft_dq: bfloat16 [16384, 8192], P('ctx', 'head')
- soft_dk: bfloat16 [16384, 1024], P('ctx', 'head')
- soft_dv: bfloat16 [16384, 1024], P('ctx', 'head')
The draws below stay inside these ranges and needn't reach their ends.
Inputs may be any that keep to these rules, and one draw needn't show every extreme that they name: `log_decay`: strictly negative. `doc_lengths`: positive lengths that add up to 16384; the largest is exactly 768.
All inputs are finite; a program needn't handle non-finite values.
Results may differ from the reference program's by a relative error of at most 0.011.
Values may be sent and summed in bfloat16 or wider, within the bound.
No kernel may reach another device: no remote copies, remote signals or barrier semaphores. Data moves between devices by JAX's collectives and lax.ppermute only.
A program may use at most 128 MiB of HBM per device.

```python
import math
import jax
import jax.numpy as jnp
import numpy as np
from jax import lax

TOK_DEV = 256
DH = 128
Q_HEADS = 64
KV_HEADS = 8
LIGHTNING_HEADS = 32
SUB = 4
SEQUENCE_LENGTH = 16384
MOST = 768
DOCS = 32
N_CTX = 64


def draw_lin_query(key, part):
    parallel_flows = jax.random.split(jax.random.fold_in(key, 101), 3)
    head_pos = jnp.arange(LIGHTNING_HEADS, dtype=jnp.float32)
    rising = 1.0 + 2.0 * head_pos / max(LIGHTNING_HEADS - 1, 1)
    column_scale = jnp.exp(jax.random.uniform(parallel_flows[1], (LIGHTNING_HEADS, DH), minval=0.0, maxval=jnp.log(4.0)))
    row_scale = jnp.exp(jax.random.uniform(parallel_flows[2], (SEQUENCE_LENGTH, 1, 1), minval=0.0, maxval=jnp.log(3.0)))
    base_draw = jnp.clip(jax.random.normal(parallel_flows[0], (SEQUENCE_LENGTH, LIGHTNING_HEADS, DH)), -4.0, 4.0)
    output_values = base_draw * rising[None, :, None] * column_scale[None] * row_scale
    return output_values.reshape(SEQUENCE_LENGTH, LIGHTNING_HEADS * DH).astype(jnp.bfloat16)


def draw_log_decay(key, part):
    parallel_flows = jax.random.split(jax.random.fold_in(key, 202), 7)
    fast_cut = 5
    fast_heads = jax.random.randint(parallel_flows[0], (LIGHTNING_HEADS,), 0, 10) < fast_cut
    fast_rate = jnp.exp(jax.random.uniform(parallel_flows[1], (LIGHTNING_HEADS,), minval=jnp.log(0.03), maxval=jnp.log(0.08)))
    slow_rate = jax.random.uniform(parallel_flows[2], (LIGHTNING_HEADS,), minval=0.2, maxval=0.6) / SEQUENCE_LENGTH
    per_head_rate = jnp.where(fast_heads, fast_rate, slow_rate)
    block_multiplier = jnp.exp(jax.random.uniform(parallel_flows[3], (LIGHTNING_HEADS, SEQUENCE_LENGTH // TOK_DEV, 1), minval=jnp.log(0.5), maxval=jnp.log(2.0)))
    block_multiplier = jnp.broadcast_to(block_multiplier, (LIGHTNING_HEADS, SEQUENCE_LENGTH // TOK_DEV, TOK_DEV)).reshape(LIGHTNING_HEADS, SEQUENCE_LENGTH)
    local_multiplier = jax.random.uniform(parallel_flows[4], (LIGHTNING_HEADS, SEQUENCE_LENGTH), minval=0.5, maxval=1.5)
    spike_positions = jax.random.randint(parallel_flows[5], (3,), 0, SEQUENCE_LENGTH)
    spike_applied = jnp.any(jnp.arange(SEQUENCE_LENGTH)[:, None] == spike_positions[None, :], axis=1)
    spike_retained = jax.random.uniform(parallel_flows[6], (LIGHTNING_HEADS, SEQUENCE_LENGTH), minval=0.55, maxval=0.8)
    output_values = -per_head_rate[:, None] * block_multiplier * local_multiplier + jnp.where(spike_applied[None, :], jnp.log(spike_retained), 0.0)
    return output_values.astype(jnp.float32)


def softmax_pair(key):
    parallel_flows = jax.random.split(jax.random.fold_in(key, 303), 2)
    query_draw = jnp.clip(jax.random.normal(parallel_flows[0], (SEQUENCE_LENGTH, Q_HEADS, DH)), -4.0, 4.0)
    key_draw = jnp.clip(jax.random.normal(parallel_flows[1], (SEQUENCE_LENGTH, KV_HEADS, DH)), -4.0, 4.0)
    return (query_draw.reshape(SEQUENCE_LENGTH, Q_HEADS * DH), key_draw.reshape(SEQUENCE_LENGTH, KV_HEADS * DH))


def draw_soft_query(key, part):
    return softmax_pair(key)[0].astype(jnp.bfloat16)


def draw_soft_keys(key, part):
    return softmax_pair(key)[1].astype(jnp.bfloat16)


def spiked(values, own_key, source, target, parts, factor):
    def block_of(dim):
        return (jnp.arange(values.shape[dim]) // (values.shape[dim] // parts)).reshape((-1,) + (1,) * (values.ndim - 1 - dim))

    near = jax.random.permutation(own_key, parts)[block_of(target)]
    other_side = (block_of(target) + parts // 2) % parts
    return jnp.where((block_of(source) == near) | (block_of(source) == other_side), factor * values, values)


def steps_of(rng, dims, cuts, least, largest):
    level = 1.0
    for axis_at, blocks in cuts:
        steps = jax.random.uniform(jax.random.fold_in(jax.random.fold_in(rng, 6), axis_at), (blocks,), jnp.float32, least / len(cuts), largest / len(cuts))
        level = level * jnp.repeat(jnp.exp(steps), dims[axis_at] // blocks).reshape((-1,) + (1,) * (len(dims) - 1 - axis_at))
    return level


def split_up(amount, total, limit, lean):
    portions = [(1 << 20) // math.isqrt(grade ** lean) + 1 for grade in range(2, amount + 1)]
    surplus, holding = total - limit - (amount - 1), [1] * (amount - 1)
    while surplus > 0:
        free = [i for i in range(amount - 1) if holding[i] < limit]
        pool, left = sum([portions[i] for i in free]), surplus
        for i in free:
            addition = min(limit - holding[i], max(1, left * portions[i] // pool), surplus)
            holding[i] = holding[i] + addition
            surplus = surplus - addition
    return np.array([limit] + holding)


def uneven(stream_key, amount, total, most, lean):
    if amount == 2:
        one = jax.random.randint(stream_key, (), max(1, total - most), min(most, total - 1) + 1)
        return jnp.stack([one, total - one])
    sizes = jnp.asarray(split_up(amount, total, most, lean), jnp.int32)
    twos = (amount - 1) // 2
    source_of, sink = sizes[1:1 + 2 * twos:2], sizes[2:2 + 2 * twos:2]
    slack = jnp.minimum(source_of - 1, most - sink)
    shifted = jax.random.randint(jax.random.fold_in(stream_key, 1), (twos,), 0, 1 << 20) % (slack + 1)
    sizes = sizes.at[1:1 + 2 * twos:2].set(source_of - shifted).at[2:2 + 2 * twos:2].set(sink + shifted)
    return sizes[jax.random.permutation(jax.random.fold_in(stream_key, 2), amount)]


def gaussian(key, shape, width, bound, pieces=(), held_as=jnp.bfloat16):
    level = steps_of(key, shape, pieces, -0.22, 0.18) if pieces else 1.0
    drawn = jax.random.normal(key, shape, jnp.float32) * width * level
    return jnp.minimum(jnp.maximum(drawn, -bound), bound).astype(held_as)


def noise_with(stream_key, shape, width, most, shards, heavy, kind=jnp.bfloat16):
    values = width * jax.random.normal(stream_key, shape, jnp.float32)
    if shards:
        values = values * steps_of(stream_key, shape, shards, -0.22, 0.18)
    return jnp.clip(spiked(values, jax.random.fold_in(stream_key, 3), *heavy), -most, most).astype(kind)


def setup_inputs(seed: int = 0) -> dict:
    keys = jax.random.split(jax.random.key(seed), 14)
    return {
        "lin_query": draw_lin_query(jax.random.fold_in(keys[13], 71), 0),
        "lin_keys": gaussian(keys[1], (SEQUENCE_LENGTH, LIGHTNING_HEADS * DH), 1.0, 6.0, ((0, 64), (1, 8))),
        "lin_values": gaussian(keys[2], (SEQUENCE_LENGTH, LIGHTNING_HEADS * DH), 1.0, 6.0, ((0, 64), (1, 8))),
        "lin_grad": gaussian(keys[3], (SEQUENCE_LENGTH, LIGHTNING_HEADS * DH), 1.0, 6.0, ((0, 64), (1, 8))),
        "norm_gain": jnp.clip(1.0 + 0.18 * jax.random.normal(keys[4], (LIGHTNING_HEADS * DH,), jnp.float32), 0.1, 1.9),
        "log_decay": draw_log_decay(jax.random.fold_in(keys[13], 71), 0),
        "state_in": gaussian(keys[6], (N_CTX, LIGHTNING_HEADS, DH, DH), 16.0, 96.0, ((0, 64), (1, 8))),
        "soft_query": draw_soft_query(jax.random.fold_in(keys[13], 71), 0),
        "soft_keys": draw_soft_keys(jax.random.fold_in(keys[13], 71), 0),
        "soft_values": gaussian(keys[9], (SEQUENCE_LENGTH, KV_HEADS * DH), 1.0, 6.0, ((0, 64), (1, 8))),
        "soft_grad": gaussian(keys[10], (SEQUENCE_LENGTH, Q_HEADS * DH), 1.0, 6.0, ((0, 64), (1, 8))),
        "projections": noise_with(keys[11], (2, LIGHTNING_HEADS * DH, KV_HEADS * DH), (LIGHTNING_HEADS * DH) ** -0.5, 0.125, ((2, 8),), (2, 1, 8, 2.0)),
        "doc_lengths": uneven(keys[12], DOCS, SEQUENCE_LENGTH, MOST, 2).astype(jnp.int32),
    }


epsilon = 1e-06
precise = lax.Precision.HIGHEST

def document_of(positions, doc_lengths):
    doc_ends = jnp.cumsum(doc_lengths).astype(jnp.int32)
    return lax.optimization_barrier(jnp.sum((doc_ends[None, :] <= positions[:, None]).astype(jnp.int32), axis=1))

def decay_weights(log_block):
    running = jnp.cumsum(log_block, axis=1)
    position = jnp.arange(log_block.shape[1], dtype=jnp.int32)
    before = position[:, None] >= position[None, :]
    log_gap = running[:, :, None] - running[:, None, :]
    weights = jnp.where(before[None], jnp.exp(jnp.minimum(log_gap, 0.0)), 0.0)
    return (running, weights)

def lin_first(query_blk, key_blk, value_blk, grad_blk, gain, log_block, state_blk):
    running, weights = decay_weights(log_block)
    query_f = query_blk.astype(jnp.float32)
    key_f = key_blk.astype(jnp.float32)
    value_f = value_blk.astype(jnp.float32)
    state_f = state_blk.astype(jnp.float32)
    near_terms = (jnp.einsum('thd,shd->hts', query_f, key_f, precision=precise) * weights).astype(jnp.bfloat16)
    near_f = lax.optimization_barrier(near_terms).astype(jnp.float32)
    growth = jnp.exp(running).T[:, :, None]
    scaled_low = (query_f * growth).astype(jnp.bfloat16)
    scaled = lax.optimization_barrier(scaled_low).astype(jnp.float32)
    inside = jnp.einsum('hts,shd->thd', near_f, value_f, precision=precise)
    carried = jnp.einsum('thd,hde->the', scaled, state_f, precision=precise)
    lin_out = (inside + carried) / DH
    gated = gain[None] * grad_blk.astype(jnp.float32)
    features = LIGHTNING_HEADS * DH
    squares = lax.optimization_barrier(jnp.sum(lin_out * lin_out, axis=(1, 2)))
    cross_term = lax.optimization_barrier(jnp.sum(gated * lin_out, axis=(1, 2)))
    spread = jnp.sqrt(squares / features + epsilon)
    out_grad = (gated / spread[:, None, None] - lin_out * (cross_term / (features * spread ** 3))[:, None, None]).astype(jnp.bfloat16)
    out_grad_f = lax.optimization_barrier(out_grad).astype(jnp.float32)
    far_terms = (jnp.einsum('the,she->hts', out_grad_f, value_f, precision=precise) * weights).astype(jnp.bfloat16)
    far_f = lax.optimization_barrier(far_terms).astype(jnp.float32)
    grad_query = (jnp.einsum('hts,shd->thd', far_f, key_f, precision=precise) + growth * jnp.einsum('the,hde->thd', out_grad_f, state_f, precision=precise)) / DH
    summary = jnp.einsum('thd,the->hde', scaled, out_grad_f, precision=precise).astype(jnp.bfloat16)
    return (grad_query.astype(jnp.bfloat16), out_grad, summary, running[:, -1])

def lin_second(query_blk, key_blk, value_blk, out_grad, log_block, after_state):
    running, weights = decay_weights(log_block)
    query_f = query_blk.astype(jnp.float32)
    key_f = key_blk.astype(jnp.float32)
    value_f = value_blk.astype(jnp.float32)
    out_grad_f = out_grad.astype(jnp.float32)
    after_low = lax.optimization_barrier(after_state.astype(jnp.bfloat16)).astype(jnp.float32)
    near_terms = (jnp.einsum('thd,shd->hts', query_f, key_f, precision=precise) * weights).astype(jnp.bfloat16)
    near_f = lax.optimization_barrier(near_terms).astype(jnp.float32)
    far_terms = (jnp.einsum('the,she->hts', out_grad_f, value_f, precision=precise) * weights).astype(jnp.bfloat16)
    far_f = lax.optimization_barrier(far_terms).astype(jnp.float32)
    tail_decay = jnp.exp(running[:, -1:] - running).T[:, :, None]
    grad_key = (jnp.einsum('hst,shd->thd', far_f, query_f, precision=precise) + tail_decay * jnp.einsum('the,hde->thd', value_f, after_low, precision=precise)) / DH
    grad_value = (jnp.einsum('hst,she->the', near_f, out_grad_f, precision=precise) + tail_decay * jnp.einsum('thd,hde->the', key_f, after_low, precision=precise)) / DH
    return (grad_key.astype(jnp.bfloat16), grad_value.astype(jnp.bfloat16))

def lightning_reference(lin_query, lin_keys, lin_values, cotangent, norm_gain, log_decay, state_in):
    block_total = SEQUENCE_LENGTH // TOK_DEV
    shaped = (block_total, TOK_DEV, LIGHTNING_HEADS, DH)
    query_all = lin_query.reshape(shaped)
    key_all = lin_keys.reshape(shaped)
    value_all = lin_values.reshape(shaped)
    grad_all = cotangent.reshape(shaped)
    log_all = log_decay.reshape(LIGHTNING_HEADS, block_total, TOK_DEV).transpose(1, 0, 2)
    gain = norm_gain.reshape(LIGHTNING_HEADS, DH)

    def first_pass(blocks_in):
        return lin_first(blocks_in[0], blocks_in[1], blocks_in[2], blocks_in[3], gain, blocks_in[4], blocks_in[5])
    grad_query, out_grad, summary, totals = lax.map(first_pass, (query_all, key_all, value_all, grad_all, log_all, state_in))

    def backward_step(after_sum, blocks_in):
        block_sum, total_log = blocks_in
        return (block_sum.astype(jnp.float32) + jnp.exp(total_log)[:, None, None] * after_sum, after_sum)
    start_state = jnp.zeros((LIGHTNING_HEADS, DH, DH), jnp.float32)
    last_state, after_all = lax.scan(backward_step, start_state, (summary, totals), reverse=True)

    def second_pass(blocks_in):
        return lin_second(blocks_in[0], blocks_in[1], blocks_in[2], blocks_in[3], blocks_in[4], blocks_in[5])
    grad_key, grad_value = lax.map(second_pass, (query_all, key_all, value_all, out_grad, log_all, after_all))
    flat = (SEQUENCE_LENGTH, LIGHTNING_HEADS * DH)
    return (grad_query.reshape(flat), grad_key.reshape(flat), grad_value.reshape(flat))

def softmax_reference(soft_query, soft_keys, soft_values, soft_grad, doc_lengths):
    group_size = Q_HEADS // KV_HEADS
    window_rows = SUB * TOK_DEV
    margin = (SUB - 1) * TOK_DEV
    score_scale = DH ** (-0.5)
    padding = jnp.zeros((margin, KV_HEADS * DH), jnp.bfloat16)
    key_pad = jnp.concatenate([padding, soft_keys], axis=0)
    value_pad = jnp.concatenate([padding, soft_values], axis=0)

    def one_block(running_sums, block_index):
        acc_key, acc_value = running_sums
        first_row = (block_index * TOK_DEV).astype(jnp.int32)
        query_blk = lax.dynamic_slice_in_dim(soft_query, first_row, TOK_DEV, 0).reshape(TOK_DEV, KV_HEADS, group_size, DH).astype(jnp.float32)
        grad_blk = lax.dynamic_slice_in_dim(soft_grad, first_row, TOK_DEV, 0).reshape(TOK_DEV, KV_HEADS, group_size, DH).astype(jnp.float32)
        key_win = lax.dynamic_slice_in_dim(key_pad, first_row, window_rows, 0).reshape(window_rows, KV_HEADS, DH).astype(jnp.float32)
        value_win = lax.dynamic_slice_in_dim(value_pad, first_row, window_rows, 0).reshape(window_rows, KV_HEADS, DH).astype(jnp.float32)
        query_pos = first_row + jnp.arange(TOK_DEV, dtype=jnp.int32)
        key_pos = first_row - margin + jnp.arange(window_rows, dtype=jnp.int32)
        visible = (key_pos[None, :] <= query_pos[:, None]) & (key_pos[None, :] >= 0) & (document_of(key_pos, doc_lengths)[None, :] == document_of(query_pos, doc_lengths)[:, None])
        scores = jnp.einsum('tkgd,skd->kgts', query_blk, key_win, precision=precise) * score_scale
        scores = jnp.where(visible, scores, -1e+30)
        highest = lax.optimization_barrier(jnp.max(scores, axis=-1, keepdims=True))
        raised = jnp.where(visible, jnp.exp(scores - highest), 0.0)
        attention = raised / lax.optimization_barrier(jnp.sum(raised, axis=-1, keepdims=True))
        prob_low = lax.optimization_barrier(attention.astype(jnp.bfloat16)).astype(jnp.float32)
        output = jnp.einsum('kgts,skd->tkgd', prob_low, value_win, precision=precise)
        row_delta = lax.optimization_barrier(jnp.sum(grad_blk * output, axis=-1))
        grad_probs = jnp.einsum('tkgd,skd->kgts', grad_blk, value_win, precision=precise)
        dscore = (attention * (grad_probs - jnp.transpose(row_delta, (1, 2, 0))[..., None]) * score_scale).astype(jnp.bfloat16)
        dscore_f = lax.optimization_barrier(dscore).astype(jnp.float32)
        grad_query = jnp.einsum('kgts,skd->tkgd', dscore_f, key_win, precision=precise).astype(jnp.bfloat16).reshape(TOK_DEV, Q_HEADS * DH)
        part_key = jnp.einsum('kgts,tkgd->skd', dscore_f, query_blk, precision=precise)
        part_value = jnp.einsum('kgts,tkgd->skd', prob_low, grad_blk, precision=precise)
        acc_key = lax.dynamic_update_slice_in_dim(acc_key, lax.dynamic_slice_in_dim(acc_key, first_row, window_rows, 0) + part_key, first_row, 0)
        acc_value = lax.dynamic_update_slice_in_dim(acc_value, lax.dynamic_slice_in_dim(acc_value, first_row, window_rows, 0) + part_value, first_row, 0)
        return ((acc_key, acc_value), grad_query)
    zero_rows = jnp.zeros((SEQUENCE_LENGTH + margin, KV_HEADS, DH), jnp.float32)
    sums_out, grads = lax.scan(one_block, (zero_rows, zero_rows), jnp.arange(N_CTX, dtype=jnp.int32))
    soft_dq = grads.reshape(SEQUENCE_LENGTH, Q_HEADS * DH)
    soft_dk = sums_out[0][margin:].reshape(SEQUENCE_LENGTH, KV_HEADS * DH).astype(jnp.bfloat16)
    soft_dv = sums_out[1][margin:].reshape(SEQUENCE_LENGTH, KV_HEADS * DH).astype(jnp.bfloat16)
    return (soft_dq, soft_dk, soft_dv)

def reference(lin_query, lin_keys, lin_values, lin_grad, norm_gain, log_decay, state_in, soft_query, soft_keys, soft_values, soft_grad, projections, doc_lengths):
    soft_dq, soft_dk, soft_dv = softmax_reference(soft_query, soft_keys, soft_values, soft_grad, doc_lengths)
    stacked = jnp.stack([soft_dk, soft_dv], axis=1).astype(jnp.float32)
    carried_back = jnp.einsum('tck,cfk->tf', stacked, projections.astype(jnp.float32), precision=precise)
    cotangent = lin_grad.astype(jnp.float32) + carried_back
    lin_dq, lin_dk, lin_dv = lightning_reference(lin_query, lin_keys, lin_values, cotangent, norm_gain, log_decay, state_in)
    return (lin_dq, lin_dk, lin_dv, soft_dq, soft_dk, soft_dv)
```

```python
import functools
import math

import jax
import jax.numpy as jnp
from jax import lax
from jax.experimental import pallas as pl
from jax.experimental.pallas import tpu as pltpu
from jax.sharding import PartitionSpec as P

DH = 128
Q_HEADS = 64
KV_HEADS = 8
GROUP = Q_HEADS // KV_HEADS
LIGHTNING_HEADS = 32
FEATURES = LIGHTNING_HEADS * DH
SUB = 4
QUAD = 4
epsilon = 1e-06

F32 = jnp.float32
BF16 = jnp.bfloat16
NT = (((1,), (1,)), ((), ()))
NN = (((1,), (0,)), ((), ()))
TN = (((0,), (0,)), ((), ()))
VMEM_LIMIT = 48 * 1024 * 1024


def mm(a, b, dims=NN):
    return lax.dot_general(a, b, dims, preferred_element_type=F32)


def iota2(shape, dim):
    return lax.broadcasted_iota(jnp.int32, shape, dim)


def to_column(row):
    n = row.shape[1]
    return jnp.sum(jnp.where(iota2((n, n), 0) == iota2((n, n), 1), row, 0.0), axis=1, keepdims=True)


def to_row(column):
    n = column.shape[0]
    return jnp.sum(jnp.where(iota2((n, n), 0) == iota2((n, n), 1), column, 0.0), axis=0, keepdims=True)


def decay_sums(log_row):
    n = log_row.shape[1]
    first, second = iota2((n, n), 0), iota2((n, n), 1)
    g_col = jnp.sum(jnp.where(second <= first, log_row, 0.0), axis=1, keepdims=True)
    return g_col, to_row(g_col)


def softmax_kernel(
    length, base_ref, lens_ref, q_ref, do_ref, kv3, kv2, kv1, kv0,
    dq_ref, part3, part2, part1, own, k_win, v_win, k_t, bias, acc_k, acc_v,
):
    step = pl.program_id(0)
    window = SUB * length
    scale = DH ** -0.5

    @pl.when(step == 0)
    def _():
        for slot, kv in enumerate((kv3, kv2, kv1, kv0)):
            rows = slice(slot * length, (slot + 1) * length)
            k_win[rows, :] = kv[0]
            v_win[rows, :] = kv[1]
            k_t[:, rows] = kv[0].astype(F32).T.astype(BF16)
        docs = lens_ref.shape[1]
        lens = jnp.where(iota2((docs, docs), 1) <= iota2((docs, docs), 0), lens_ref[...], 0)
        ends = jnp.sum(lens, axis=1, keepdims=True)
        base = base_ref[0]
        t_row = base + iota2((docs, length), 1)
        start = jnp.max(jnp.where(ends <= t_row, ends, 0), axis=0, keepdims=True)
        s_pos = base - (SUB - 1) * length + iota2((window, length), 0)
        t_pos = base + iota2((window, length), 1)
        visible = (s_pos <= t_pos) & (s_pos >= start)
        bias[...] = jnp.where(visible, 0.0, -1e30)
        acc_k[...] = jnp.zeros_like(acc_k)
        acc_v[...] = jnp.zeros_like(acc_v)

    q = q_ref[...]
    do = do_ref[...]
    scores = mm(k_win[...], q, NT) * (scale * math.log2(math.e)) + bias[...]
    highest = jnp.max(scores, axis=0, keepdims=True)
    raised = jnp.exp2(scores - highest)
    inverse = 1.0 / jnp.sum(raised, axis=0, keepdims=True)
    prob = raised * inverse
    prob_low = prob.astype(BF16)
    grad_probs = mm(v_win[...], do, NT)
    delta = jnp.sum(prob_low.astype(F32) * grad_probs, axis=0, keepdims=True)
    dscore = (prob * ((grad_probs - delta) * scale)).astype(BF16)
    acc_v[...] += mm(prob_low, do)
    acc_k[...] += mm(dscore, q)
    dq_ref[...] = mm(k_t[...], dscore).T.astype(BF16)

    @pl.when(step == pl.num_programs(0) - 1)
    def _():
        for slot, out in enumerate((part3, part2, part1, own)):
            rows = slice(slot * length, (slot + 1) * length)
            out[:, :DH] = acc_k[rows, :].astype(out.dtype)
            out[:, DH:] = acc_v[rows, :].astype(out.dtype)


def softmax_call(base, lens, q, do, windows):
    length = q.shape[0]
    whole = lambda *shape: pl.BlockSpec(shape, lambda j: (0,) * len(shape))
    per_head = pl.BlockSpec((length, DH), lambda j: (0, j))
    window = SUB * length
    pair = jax.ShapeDtypeStruct((length, 2 * DH), BF16)
    return pl.pallas_call(
        functools.partial(softmax_kernel, length),
        out_shape=(
            jax.ShapeDtypeStruct(q.shape, BF16), pair, pair, pair,
            jax.ShapeDtypeStruct((length, 2 * DH), F32),
        ),
        grid=(GROUP,),
        in_specs=[
            pl.BlockSpec(memory_space=pltpu.SMEM), whole(1, lens.shape[1]), per_head, per_head,
        ] + [whole(2, length, DH)] * SUB,
        out_specs=(per_head,) + (whole(length, 2 * DH),) * SUB,
        scratch_shapes=[
            pltpu.VMEM((window, DH), BF16), pltpu.VMEM((window, DH), BF16),
            pltpu.VMEM((DH, window), BF16), pltpu.VMEM((window, length), F32),
            pltpu.VMEM((window, DH), F32), pltpu.VMEM((window, DH), F32),
        ],
        compiler_params=pltpu.CompilerParams(vmem_limit_bytes=VMEM_LIMIT),
        cost_estimate=pl.CostEstimate(
            flops=10 * GROUP * window * length * DH * 4, bytes_accessed=4 * 1024 * 1024,
            transcendentals=GROUP * window * length,
        ),
        name="softmax_backward",
    )(base, lens, q, do, *windows)


def forward_kernel(block_ref, q_ref, k_ref, v_ref, log_ref, state_ref, out_ref):
    head = pl.program_id(0)
    length = q_ref.shape[0]
    g_col, g_row = decay_sums(log_ref[pl.ds(head, 1), :])
    causal = iota2((length, length), 0) >= iota2((length, length), 1)
    weights = jnp.where(causal, jnp.exp(jnp.minimum(g_col - g_row, 0.0)), 0.0)
    near = (mm(q_ref[...], k_ref[...], NT) * weights).astype(BF16)
    scaled = (q_ref[...].astype(F32) * jnp.exp(g_col)).astype(BF16)
    out_ref[...] = (mm(near, v_ref[...]) + mm(scaled, state_ref[0, 0])) * (1.0 / DH)


def per_head_spec(length):
    return pl.BlockSpec((length, DH), lambda h, b: (0, h))


def state_spec():
    return pl.BlockSpec((1, 1, DH, DH), lambda h, b: (0, h, 0, 0))


def log_spec(heads, length):
    return pl.BlockSpec((heads, length), lambda h, b: (0, b[0]))


def forward_call(block, q, k, v, log_decay, state):
    length, heads = q.shape[0], q.shape[1] // DH
    wide = per_head_spec(length)
    return pl.pallas_call(
        forward_kernel,
        out_shape=jax.ShapeDtypeStruct(q.shape, F32),
        grid_spec=pltpu.PrefetchScalarGridSpec(
            num_scalar_prefetch=1, grid=(heads,),
            in_specs=[wide, wide, wide, log_spec(heads, length), state_spec()],
            out_specs=wide,
        ),
        cost_estimate=pl.CostEstimate(
            flops=heads * length * DH * (4 * length + 2 * DH) * 8, bytes_accessed=2 * 1024 * 1024,
            transcendentals=heads * length * length,
        ),
        name="lightning_forward",
    )(block, q, k, v, log_decay, state)


def cotangent_kernel(dkv_ref, proj_ref, grad_ref, gain_ref, out_ref, gated_ref, stats_ref):
    total = grad_ref[...].astype(F32)
    for g in range(KV_HEADS):
        for side in range(2):
            total += mm(dkv_ref[g, :, side * DH:(side + 1) * DH], proj_ref[side, g], NT)
    gated = gain_ref[...] * total
    gated_ref[...] = gated
    out = out_ref[...]
    squares = to_row(jnp.sum(out * out, axis=1, keepdims=True))
    cross = to_row(jnp.sum(gated * out, axis=1, keepdims=True))
    rows = iota2(stats_ref.shape, 0)
    stats_ref[...] = jnp.where(rows == 0, squares, jnp.where(rows == 1, cross, 0.0))


def cotangent_call(dkv, proj, grad, gain, out):
    length, width = grad.shape
    return pl.pallas_call(
        cotangent_kernel,
        out_shape=(
            jax.ShapeDtypeStruct((length, width), F32), jax.ShapeDtypeStruct((8, length), F32),
        ),
        compiler_params=pltpu.CompilerParams(vmem_limit_bytes=VMEM_LIMIT),
        name="cotangent",
    )(dkv, proj, grad, gain, out)


def dout_kernel(block_ref, stats_ref, gated_ref, out_ref, q_ref, log_ref, dout_ref, summary_ref):
    head = pl.program_id(0)
    g_col, _ = decay_sums(log_ref[pl.ds(head, 1), :])
    squares = to_column(stats_ref[0:1, :])
    cross = to_column(stats_ref[1:2, :])
    spread = jnp.sqrt(squares * (1.0 / FEATURES) + epsilon)
    inverse = 1.0 / spread
    factor = cross * (inverse * inverse * inverse) * (1.0 / FEATURES)
    dout = (gated_ref[...] * inverse - out_ref[...] * factor).astype(BF16)
    dout_ref[...] = dout
    scaled = (q_ref[...].astype(F32) * jnp.exp(g_col)).astype(BF16)
    summary_ref[0] = mm(scaled, dout, TN).astype(BF16)


def dout_call(block, stats, gated, out, q, log_decay):
    length, heads = q.shape[0], q.shape[1] // DH
    wide = per_head_spec(length)
    return pl.pallas_call(
        dout_kernel,
        out_shape=(jax.ShapeDtypeStruct(q.shape, BF16), jax.ShapeDtypeStruct((heads, DH, DH), BF16)),
        grid_spec=pltpu.PrefetchScalarGridSpec(
            num_scalar_prefetch=1, grid=(heads,),
            in_specs=[
                pl.BlockSpec((8, length), lambda h, b: (0, 0)), wide, wide, wide,
                log_spec(heads, length),
            ],
            out_specs=(wide, pl.BlockSpec((1, DH, DH), lambda h, b: (h, 0, 0))),
        ),
        name="dout_summary",
    )(block, stats, gated, out, q, log_decay)


def near_far_kernel(
    block_ref, q_ref, k_ref, v_ref, dout_ref, log_ref, state_ref, dq_ref, dk_ref, dv_ref
):
    head = pl.program_id(0)
    length = q_ref.shape[0]
    g_col, g_row = decay_sums(log_ref[pl.ds(head, 1), :])
    first, second = iota2((length, length), 0), iota2((length, length), 1)
    gap = g_col - g_row
    weights = jnp.where(first >= second, jnp.exp(jnp.minimum(gap, 0.0)), 0.0)
    turned = jnp.where(second >= first, jnp.exp(jnp.minimum(-gap, 0.0)), 0.0)
    q, k, v, dout = q_ref[...], k_ref[...], v_ref[...], dout_ref[...]
    far = (mm(dout, v, NT) * weights).astype(BF16)
    far_turned = (mm(v, dout, NT) * turned).astype(BF16)
    near_turned = (mm(k, q, NT) * turned).astype(BF16)
    dq = mm(far, k) + jnp.exp(g_col) * mm(dout, state_ref[0, 0], NT)
    dq_ref[...] = (dq * (1.0 / DH)).astype(BF16)
    dk_ref[...] = mm(far_turned, q)
    dv_ref[...] = mm(near_turned, dout)


def near_far_call(block, q, k, v, dout, log_decay, state):
    length, heads = q.shape[0], q.shape[1] // DH
    wide = per_head_spec(length)
    return pl.pallas_call(
        near_far_kernel,
        out_shape=(
            jax.ShapeDtypeStruct(q.shape, BF16), jax.ShapeDtypeStruct(q.shape, F32),
            jax.ShapeDtypeStruct(q.shape, F32),
        ),
        grid_spec=pltpu.PrefetchScalarGridSpec(
            num_scalar_prefetch=1, grid=(heads,),
            in_specs=[wide, wide, wide, wide, log_spec(heads, length), state_spec()],
            out_specs=(wide, wide, wide),
        ),
        cost_estimate=pl.CostEstimate(
            flops=heads * length * DH * (12 * length + 2 * DH) * 8, bytes_accessed=4 * 1024 * 1024,
            transcendentals=2 * heads * length * length,
        ),
        name="near_far",
    )(block, q, k, v, dout, log_decay, state)


def last_kernel(block_ref, k_ref, v_ref, dk_ref, dv_ref, after_ref, log_ref, dk_out, dv_out):
    head = pl.program_id(0)
    length = k_ref.shape[0]
    log_row = log_ref[pl.ds(head, 1), :]
    first, second = iota2((length, length), 0), iota2((length, length), 1)
    tail = jnp.exp(jnp.sum(jnp.where(second > first, log_row, 0.0), axis=1, keepdims=True))
    after = after_ref[0]
    dk_out[...] = ((dk_ref[...] + tail * mm(v_ref[...], after, NT)) * (1.0 / DH)).astype(BF16)
    dv_out[...] = ((dv_ref[...] + tail * mm(k_ref[...], after)) * (1.0 / DH)).astype(BF16)


def last_call(block, k, v, dk, dv, after, log_decay):
    length, heads = k.shape[0], k.shape[1] // DH
    wide = per_head_spec(length)
    return pl.pallas_call(
        last_kernel,
        out_shape=(jax.ShapeDtypeStruct(k.shape, BF16), jax.ShapeDtypeStruct(k.shape, BF16)),
        grid_spec=pltpu.PrefetchScalarGridSpec(
            num_scalar_prefetch=1, grid=(heads,),
            in_specs=[
                wide, wide, wide, wide, pl.BlockSpec((1, DH, DH), lambda h, b: (h, 0, 0)),
                log_spec(heads, length),
            ],
            out_specs=(wide, wide),
        ),
        name="last",
    )(block, k, v, dk, dv, after, log_decay)


def total_kernel(weight_ref, blocks_ref, total_ref):
    total = jnp.zeros(total_ref.shape, F32)
    for z in range(QUAD):
        total += weight_ref[z] * blocks_ref[z].astype(F32)
    total_ref[...] = total.astype(total_ref.dtype)


def after_kernel(inner_ref, carry_ref, leave_ref, blocks_ref, totals_ref, after_ref):
    carry = jnp.zeros(after_ref.shape[1:], F32)
    for g in range(totals_ref.shape[0]):
        carry += carry_ref[g] * totals_ref[g].astype(F32)
    for z in range(QUAD):
        after = leave_ref[z] * carry
        for later in range(z + 1, QUAD):
            after += inner_ref[z, later] * blocks_ref[later].astype(F32)
        after_ref[z] = after.astype(BF16)


def state_weights(log_decay, length, device):
    place = device % QUAD
    group = device // QUAD
    row = lax.dynamic_slice_in_dim(log_decay, place, 1, 0)
    gamma = jnp.sum(row.reshape(-1, length), axis=1)
    count = gamma.shape[0]
    block = jnp.arange(count, dtype=jnp.int32)
    groups = count // QUAD
    quad = jnp.arange(QUAD, dtype=jnp.int32)
    start = group * QUAD

    def factor(low, high):
        inside = (block > low[..., None]) & (block < high[..., None])
        return jnp.exp(jnp.sum(jnp.where(inside, gamma, 0.0), axis=-1))

    enter = factor(jnp.broadcast_to(start - 1, (QUAD,)), start + quad)
    inner = factor((start + quad)[:, None], (start + quad)[None, :])
    leave = factor(start + quad, jnp.broadcast_to(start + QUAD, (QUAD,)))
    later = jnp.arange(groups, dtype=jnp.int32)
    carry = factor(jnp.broadcast_to(start + QUAD - 1, (groups,)), later * QUAD)
    carry = jnp.where(later > group, carry, 0.0)
    return enter, inner, leave, carry


def after_states(summary, weights):
    enter, inner, leave, carry = weights
    count = lax.axis_size("ctx")
    quads = [[g * QUAD + z for z in range(QUAD)] for g in range(count // QUAD)]
    strided = [[g * QUAD + z for g in range(count // QUAD)] for z in range(QUAD)]
    smem = pl.BlockSpec(memory_space=pltpu.SMEM)
    vmem = pl.BlockSpec(memory_space=pltpu.VMEM)
    blocks = lax.all_to_all(summary, "ctx", 0, 0, tiled=True, axis_index_groups=quads)
    total = pl.pallas_call(
        total_kernel, out_shape=jax.ShapeDtypeStruct((DH, DH), BF16),
        in_specs=[smem, vmem], out_specs=vmem, name="group_total",
    )(enter, blocks)
    totals = lax.all_gather(total, "ctx", axis=0, axis_index_groups=strided)
    after = pl.pallas_call(
        after_kernel, out_shape=jax.ShapeDtypeStruct((QUAD, DH, DH), BF16),
        in_specs=[smem, smem, smem, vmem, vmem], out_specs=vmem, name="after_states",
    )(inner, carry, leave, blocks, totals)
    return lax.all_to_all(after, "ctx", 0, 0, tiled=True, axis_index_groups=quads)


def passed_along(block, distance):
    devices = range(lax.axis_size("ctx"))
    route = [(i - distance, i) for i in devices if i - distance in devices]
    return lax.ppermute(block, "ctx", route)


def per_device(
    lin_query, lin_keys, lin_values, lin_grad, norm_gain, log_decay, state_in,
    soft_query, soft_keys, soft_values, soft_grad, projections, doc_lengths,
):
    length = lin_query.shape[0]
    width = lin_query.shape[1]
    device = lax.axis_index("ctx").astype(jnp.int32)
    block = device.reshape(1)

    stacked = jnp.stack([soft_keys, soft_values])
    arrived = [passed_along(stacked, offset) for offset in range(SUB - 1, 0, -1)]
    proj = projections.reshape(2, KV_HEADS, width, DH)
    proj = lax.all_to_all(proj, "head", 1, 1, tiled=True)
    weights = state_weights(log_decay, length, device)
    lin_out = forward_call(block, lin_query, lin_keys, lin_values, log_decay, state_in)

    soft_dq, part3, part2, part1, own = softmax_call(
        block * length, doc_lengths.reshape(1, -1), soft_query, soft_grad, arrived + [stacked]
    )
    summed = own
    for offset, part in ((3, part3), (2, part2), (1, part1)):
        summed = summed + passed_along(part, -offset).astype(F32)
    dkv = summed.astype(BF16)
    soft_dk, soft_dv = dkv[:, :DH], dkv[:, DH:]

    dkv_all = lax.all_gather(dkv, "head", axis=0)
    gated, stats = cotangent_call(dkv_all, proj, lin_grad, norm_gain.reshape(1, width), lin_out)
    stats = lax.psum(stats, "head")
    dout, summary = dout_call(block, stats, gated, lin_out, lin_query, log_decay)
    lin_dq, dk, dv = near_far_call(
        block, lin_query, lin_keys, lin_values, dout, log_decay, state_in
    )
    after = after_states(summary, weights)
    lin_dk, lin_dv = last_call(block, lin_keys, lin_values, dk, dv, after, log_decay)
    return (lin_dq, lin_dk, lin_dv, soft_dq, soft_dk, soft_dv)


def solution(mesh):
    in_specs = (
        P("ctx", "head"), P("ctx", "head"), P("ctx", "head"), P("ctx", "head"),
        P("head"), P("head", None), P("ctx", "head", None, None),
        P("ctx", "head"), P("ctx", "head"), P("ctx", "head"), P("ctx", "head"),
        P(None, None, "head"), P(),
    )
    out_specs = (P("ctx", "head"),) * 6
    return jax.shard_map(
        per_device, mesh=mesh, in_specs=in_specs, out_specs=out_specs, check_vma=False
    )
```

```python
import functools
import math

import jax
import jax.numpy as jnp
from jax import lax
from jax.experimental import pallas as pl
from jax.experimental.pallas import tpu as pltpu
from jax.sharding import PartitionSpec as P

DH = 128
Q_HEADS = 64
KV_HEADS = 8
GROUP = Q_HEADS // KV_HEADS
LIGHTNING_HEADS = 32
FEATURES = LIGHTNING_HEADS * DH
SUB = 4
QUAD = 4
AT_ONCE = 2
TILES = 2
epsilon = 1e-06

F32 = jnp.float32
BF16 = jnp.bfloat16
NT = (((1,), (1,)), ((), ()))
NN = (((1,), (0,)), ((), ()))
TN = (((0,), (0,)), ((), ()))
VMEM_LIMIT = 48 * 1024 * 1024


def mm(a, b, dims=NN):
    return lax.dot_general(a, b, dims, preferred_element_type=F32)


def iota2(shape, dim):
    return lax.broadcasted_iota(jnp.int32, shape, dim)


def to_column(row):
    n = row.shape[1]
    return jnp.sum(jnp.where(iota2((n, n), 0) == iota2((n, n), 1), row, 0.0), axis=1, keepdims=True)


def to_row(column):
    n = column.shape[0]
    return jnp.sum(jnp.where(iota2((n, n), 0) == iota2((n, n), 1), column, 0.0), axis=0, keepdims=True)


def decay_sums(log_row):
    n = log_row.shape[1]
    first, second = iota2((n, n), 0), iota2((n, n), 1)
    g_col = jnp.sum(jnp.where(second <= first, log_row, 0.0), axis=1, keepdims=True)
    return g_col, to_row(g_col)


def softmax_kernel(
    length, base_ref, lens_ref, q_ref, do_ref, kv3, kv2, kv1, kv0,
    dq_ref, part3, part2, part1, own, k_win, v_win, k_t, bias, acc_k, acc_v,
):
    tile, pair = pl.program_id(0), pl.program_id(1)
    first = jnp.logical_and(tile == 0, pair == 0)
    final = jnp.logical_and(tile == pl.num_programs(0) - 1, pair == pl.num_programs(1) - 1)
    rows = q_ref.shape[0]
    reach = bias.shape[0]
    scale = DH ** -0.5

    @pl.when(first)
    def _():
        for slot, kv in enumerate((kv3, kv2, kv1, kv0)):
            here = slice(slot * length, (slot + 1) * length)
            k_win[here, :] = kv[0]
            v_win[here, :] = kv[1]
            k_t[:, here] = kv[0].astype(F32).T.astype(BF16)
        acc_k[...] = jnp.zeros_like(acc_k)
        acc_v[...] = jnp.zeros_like(acc_v)

    @pl.when(pair == 0)
    def _():
        docs = lens_ref.shape[1]
        lens = jnp.where(iota2((docs, docs), 1) <= iota2((docs, docs), 0), lens_ref[...], 0)
        ends = jnp.sum(lens, axis=1, keepdims=True)
        base = base_ref[0] + tile * rows
        t_row = base + iota2((docs, rows), 1)
        start = jnp.max(jnp.where(ends <= t_row, ends, 0), axis=0, keepdims=True)
        s_pos = base - (SUB - 1) * length + iota2((reach, rows), 0)
        t_pos = base + iota2((reach, rows), 1)
        hidden = jnp.where((s_pos <= t_pos) & (s_pos >= start), 0.0, -1e30)
        for head in range(AT_ONCE):
            bias[:, head * rows:(head + 1) * rows] = hidden

    def stacked(ref):
        return jnp.concatenate([ref[:, h * DH:(h + 1) * DH] for h in range(AT_ONCE)], axis=0)

    window = pl.ds(pl.multiple_of(tile * rows, rows), reach)
    q = stacked(q_ref)
    do = stacked(do_ref)
    scores = mm(k_win[window, :], q, NT) * (scale * math.log2(math.e)) + bias[...]
    highest = jnp.max(scores, axis=0, keepdims=True)
    raised = jnp.exp2(scores - highest)
    inverse = 1.0 / jnp.sum(raised, axis=0, keepdims=True)
    grad_probs = mm(v_win[window, :], do, NT)
    delta = jnp.sum(raised * grad_probs, axis=0, keepdims=True) * inverse
    prob = raised * inverse
    dscore = (prob * (grad_probs - delta)).astype(BF16)
    acc_v[window, :] += mm(prob.astype(BF16), do)
    acc_k[window, :] += mm(dscore, q)
    dq = (mm(k_t[:, window], dscore) * scale).T
    for head in range(AT_ONCE):
        dq_ref[:, head * DH:(head + 1) * DH] = dq[head * rows:(head + 1) * rows, :].astype(BF16)

    @pl.when(final)
    def _():
        for slot, out in enumerate((part3, part2, part1, own)):
            here = slice(slot * length, (slot + 1) * length)
            out[:, :DH] = (acc_k[here, :] * scale).astype(out.dtype)
            out[:, DH:] = acc_v[here, :].astype(out.dtype)


def softmax_call(base, lens, q, do, windows):
    length = q.shape[0]
    rows = length // TILES
    whole = lambda *shape: pl.BlockSpec(shape, lambda i, j: (0,) * len(shape))
    per_pair = pl.BlockSpec((rows, AT_ONCE * DH), lambda i, j: (i, j))
    window = SUB * length
    reach = window - length + rows
    pair = jax.ShapeDtypeStruct((length, 2 * DH), BF16)
    return pl.pallas_call(
        functools.partial(softmax_kernel, length),
        out_shape=(
            jax.ShapeDtypeStruct(q.shape, BF16), pair, pair, pair,
            jax.ShapeDtypeStruct((length, 2 * DH), F32),
        ),
        grid=(TILES, GROUP // AT_ONCE),
        in_specs=[
            pl.BlockSpec(memory_space=pltpu.SMEM), whole(1, lens.shape[1]), per_pair, per_pair,
        ] + [whole(2, length, DH)] * SUB,
        out_specs=(per_pair,) + (whole(length, 2 * DH),) * SUB,
        scratch_shapes=[
            pltpu.VMEM((window, DH), BF16), pltpu.VMEM((window, DH), BF16),
            pltpu.VMEM((DH, window), BF16), pltpu.VMEM((reach, AT_ONCE * rows), F32),
            pltpu.VMEM((window, DH), F32), pltpu.VMEM((window, DH), F32),
        ],
        compiler_params=pltpu.CompilerParams(vmem_limit_bytes=VMEM_LIMIT),
        cost_estimate=pl.CostEstimate(
            flops=200 * GROUP * window * length * DH * 4, bytes_accessed=4 * 1024 * 1024,
            transcendentals=GROUP * window * length,
        ),
        name="softmax_backward",
    )(base, lens, q, do, *windows)


def forward_kernel(
    block_ref, q_ref, k_ref, v_ref, log_ref, state_ref, out_ref, scaled_ref, tail_ref
):
    head = pl.program_id(0)
    length = q_ref.shape[0]
    g_col, g_row = decay_sums(log_ref[pl.ds(head, 1), :])
    causal = iota2((length, length), 0) >= iota2((length, length), 1)
    weights = jnp.where(causal, jnp.exp(jnp.minimum(g_col - g_row, 0.0)), 0.0)
    near = (mm(q_ref[...], k_ref[...], NT) * weights).astype(BF16)
    scaled = (q_ref[...].astype(F32) * jnp.exp(g_col)).astype(BF16)
    out = (mm(near, v_ref[...]) + mm(scaled, state_ref[0, 0])) * (1.0 / DH)
    out_ref[...] = out
    scaled_ref[...] = scaled
    tail_ref[...] = jnp.broadcast_to(jnp.exp(g_col[length - 1:, :] - g_col), out.shape)


def per_head_spec(length):
    return pl.BlockSpec((length, DH), lambda h, b: (0, h))


def state_spec():
    return pl.BlockSpec((1, 1, DH, DH), lambda h, b: (0, h, 0, 0))


def log_spec(heads, length):
    return pl.BlockSpec((heads, length), lambda h, b: (0, b[0]))


def forward_call(block, q, k, v, log_decay, state):
    length, heads = q.shape[0], q.shape[1] // DH
    wide = per_head_spec(length)
    like = lambda dtype: jax.ShapeDtypeStruct(q.shape, dtype)
    return pl.pallas_call(
        forward_kernel,
        out_shape=(like(F32), like(BF16), like(F32)),
        grid_spec=pltpu.PrefetchScalarGridSpec(
            num_scalar_prefetch=1, grid=(heads,),
            in_specs=[wide, wide, wide, log_spec(heads, length), state_spec()],
            out_specs=(wide, wide, wide),
        ),
        cost_estimate=pl.CostEstimate(
            flops=heads * length * DH * (4 * length + 2 * DH) * 8, bytes_accessed=4 * 1024 * 1024,
            transcendentals=heads * length * length,
        ),
        name="lightning_forward",
    )(block, q, k, v, log_decay, state)


def cotangent_kernel(
    core_ref, own_ref, other_ref, proj_ref, grad_ref, gain_ref, out_ref, gated_ref, stats_ref
):
    core = core_ref[0]
    total = grad_ref[...].astype(F32)
    for chip in range(own_ref.shape[0]):
        for dkv_ref, g in ((own_ref, 2 * chip + core), (other_ref, 2 * chip + 1 - core)):
            for side in range(2):
                total += mm(dkv_ref[chip, :, side * DH:(side + 1) * DH], proj_ref[g, side], NT)
    gated = gain_ref[...] * total
    gated_ref[...] = gated
    out = out_ref[...]
    squares = to_row(jnp.sum(out * out, axis=1, keepdims=True))
    cross = to_row(jnp.sum(gated * out, axis=1, keepdims=True))
    rows = iota2(stats_ref.shape[1:], 0)
    stats = jnp.where(rows == 0, squares, jnp.where(rows == 1, cross, 0.0))
    for copy in range(stats_ref.shape[0]):
        stats_ref[copy] = stats


def cotangent_call(core, own, other, proj, grad, gain, out):
    vmem = pl.BlockSpec(memory_space=pltpu.VMEM)
    return pl.pallas_call(
        cotangent_kernel,
        in_specs=[pl.BlockSpec(memory_space=pltpu.SMEM)] + [vmem] * 6,
        out_shape=(
            jax.ShapeDtypeStruct(grad.shape, F32),
            jax.ShapeDtypeStruct((KV_HEADS, 8, grad.shape[0]), F32),
        ),
        compiler_params=pltpu.CompilerParams(vmem_limit_bytes=VMEM_LIMIT),
        name="cotangent",
    )(core, own, other, proj, grad, gain, out)


def dout_kernel(stats_ref, gated_ref, out_ref, scaled_ref, dout_ref, summary_ref):
    stats = stats_ref[0]
    for source in range(1, stats_ref.shape[0]):
        stats += stats_ref[source]
    inverse = 1.0 / jnp.sqrt(stats[0:1, :] * (1.0 / FEATURES) + epsilon)
    factor = stats[1:2, :] * (inverse * inverse * inverse) * (1.0 / FEATURES)
    low = (gated_ref[...] * to_column(inverse) - out_ref[...] * to_column(factor)).astype(BF16)
    dout_ref[...] = low
    for head in range(summary_ref.shape[0]):
        columns = slice(head * DH, (head + 1) * DH)
        summary_ref[head] = mm(scaled_ref[:, columns], low[:, columns], TN).astype(BF16)


def dout_call(stats, gated, out, scaled):
    return pl.pallas_call(
        dout_kernel,
        out_shape=(
            jax.ShapeDtypeStruct(out.shape, BF16),
            jax.ShapeDtypeStruct((out.shape[1] // DH, DH, DH), BF16),
        ),
        name="dout_summary",
    )(stats, gated, out, scaled)


def near_far_kernel(
    block_ref, q_ref, k_ref, v_ref, dout_ref, log_ref, state_ref, dq_ref, dk_ref, dv_ref
):
    head = pl.program_id(0)
    length = q_ref.shape[0]
    g_col, g_row = decay_sums(log_ref[pl.ds(head, 1), :])
    first, second = iota2((length, length), 0), iota2((length, length), 1)
    gap = g_col - g_row
    weights = jnp.where(first >= second, jnp.exp(jnp.minimum(gap, 0.0)), 0.0)
    turned = jnp.where(second >= first, jnp.exp(jnp.minimum(-gap, 0.0)), 0.0)
    q, k, v, dout = q_ref[...], k_ref[...], v_ref[...], dout_ref[...]
    far = (mm(dout, v, NT) * weights).astype(BF16)
    far_turned = (mm(v, dout, NT) * turned).astype(BF16)
    near_turned = (mm(k, q, NT) * turned).astype(BF16)
    dq = mm(far, k) + jnp.exp(g_col) * mm(dout, state_ref[0, 0], NT)
    dq_ref[...] = (dq * (1.0 / DH)).astype(BF16)
    dk_ref[...] = mm(far_turned, q)
    dv_ref[...] = mm(near_turned, dout)


def near_far_call(block, q, k, v, dout, log_decay, state):
    length, heads = q.shape[0], q.shape[1] // DH
    wide = per_head_spec(length)
    return pl.pallas_call(
        near_far_kernel,
        out_shape=(
            jax.ShapeDtypeStruct(q.shape, BF16), jax.ShapeDtypeStruct(q.shape, F32),
            jax.ShapeDtypeStruct(q.shape, F32),
        ),
        grid_spec=pltpu.PrefetchScalarGridSpec(
            num_scalar_prefetch=1, grid=(heads,),
            in_specs=[wide, wide, wide, wide, log_spec(heads, length), state_spec()],
            out_specs=(wide, wide, wide),
        ),
        cost_estimate=pl.CostEstimate(
            flops=heads * length * DH * (12 * length + 2 * DH) * 8, bytes_accessed=4 * 1024 * 1024,
            transcendentals=2 * heads * length * length,
        ),
        name="near_far",
    )(block, q, k, v, dout, log_decay, state)


def last_kernel(k_ref, v_ref, dk_ref, dv_ref, tail_ref, after_ref, dk_out, dv_out):
    for head in range(after_ref.shape[0]):
        at = slice(head * DH, (head + 1) * DH)
        tail = tail_ref[:, at]
        after = after_ref[head]
        dk = dk_ref[:, at] + tail * mm(v_ref[:, at], after, NT)
        dv = dv_ref[:, at] + tail * mm(k_ref[:, at], after)
        dk_out[:, at] = (dk * (1.0 / DH)).astype(BF16)
        dv_out[:, at] = (dv * (1.0 / DH)).astype(BF16)


def last_call(k, v, dk, dv, tail, after):
    return pl.pallas_call(
        last_kernel,
        out_shape=(jax.ShapeDtypeStruct(k.shape, BF16), jax.ShapeDtypeStruct(k.shape, BF16)),
        name="last",
    )(k, v, dk, dv, tail, after)


ENTER, RISE, GROUPS, ROWS, LEAVE, INNER = 0, 4, 8, 12, 16, 20


def state_weights(log_decay, length, device):
    place, group, row = device % QUAD, device // QUAD, device // (QUAD * QUAD)
    decays = lax.dynamic_slice_in_dim(log_decay, place, 1, 0)
    gamma = jnp.sum(decays.reshape(-1, length), axis=1)
    block = jnp.arange(gamma.shape[0], dtype=jnp.int32)
    quad = jnp.arange(QUAD, dtype=jnp.int32)
    first, row_first = group * QUAD, row * QUAD * QUAD
    same = lambda x: jnp.broadcast_to(x, (QUAD,))
    group_first, rows_first = row_first + quad * QUAD, quad * QUAD * QUAD
    low = jnp.concatenate(
        [same(first - 1), same(row_first - 1), same(first + QUAD - 1), same(first + QUAD - 1), first + quad,
         jnp.repeat(first + quad, QUAD)]
    )
    high = jnp.concatenate(
        [first + quad, group_first, group_first, rows_first, same(first + QUAD), jnp.tile(first + quad, QUAD)]
    )
    yes = jnp.ones((QUAD,), bool)
    used = jnp.concatenate([yes, yes, group_first > first, quad > row, yes, jnp.ones((QUAD * QUAD,), bool)])
    inside = (block[None, :] > low[:, None]) & (block[None, :] < high[:, None])
    factors = jnp.exp(jnp.sum(jnp.where(inside, gamma[None, :], 0.0), axis=1))
    return jnp.where(used, factors, 0.0)


def rise_kernel(first, weight_ref, blocks_ref, total_ref):
    total = jnp.zeros(blocks_ref.shape[1:], F32)
    for z in range(QUAD):
        total += weight_ref[first + z] * blocks_ref[z].astype(F32)
    total = total.astype(BF16)
    for z in range(QUAD):
        total_ref[z] = total


def after_kernel(weight_ref, blocks_ref, groups_ref, rows_ref, after_ref):
    carry = jnp.zeros(blocks_ref.shape[1:], F32)
    for g in range(QUAD):
        carry += weight_ref[GROUPS + g] * groups_ref[g].astype(F32)
        carry += weight_ref[ROWS + g] * rows_ref[g].astype(F32)
    for z in range(QUAD):
        after = weight_ref[LEAVE + z] * carry
        for later in range(z + 1, QUAD):
            after += weight_ref[INNER + z * QUAD + later] * blocks_ref[later].astype(F32)
        after_ref[z] = after.astype(BF16)


def after_states(summary, weights, beside):
    count = lax.axis_size("ctx")
    square = QUAD * QUAD
    every = [[g * QUAD + i for i in range(QUAD)] for g in range(count // QUAD)]
    over_groups = [
        [r * square + i * QUAD + z for i in range(QUAD)] for r in range(count // square) for z in range(QUAD)
    ]
    over_rows = [[i * square + p for i in range(QUAD)] for p in range(square)]
    smem = pl.BlockSpec(memory_space=pltpu.SMEM)
    vmem = pl.BlockSpec(memory_space=pltpu.VMEM)
    shape = jax.ShapeDtypeStruct((QUAD, DH, DH), BF16)
    swap = lambda x, groups: lax.all_to_all(x, "ctx", 0, 0, tiled=True, axis_index_groups=groups)

    def rise(first, blocks):
        return pl.pallas_call(
            functools.partial(rise_kernel, first), out_shape=shape,
            in_specs=[smem, vmem], out_specs=vmem, name="rise",
        )(weights, blocks)

    blocks = swap(summary, every)
    groups = swap(rise(ENTER, blocks), over_groups)
    risen, beside = lax.optimization_barrier((rise(RISE, groups), beside))
    rows = swap(risen, over_rows)
    after = pl.pallas_call(
        after_kernel, out_shape=shape, in_specs=[smem, vmem, vmem, vmem], out_specs=vmem, name="after_states",
    )(weights, blocks, groups, rows)
    return swap(after, every), beside


def passed_along(block, distance):
    devices = range(lax.axis_size("ctx"))
    route = [(i - distance, i) for i in devices if i - distance in devices]
    return lax.ppermute(block, "ctx", route)


def per_device(
    lin_query, lin_keys, lin_values, lin_grad, norm_gain, log_decay, state_in,
    soft_query, soft_keys, soft_values, soft_grad, projections, doc_lengths,
):
    length = lin_query.shape[0]
    width = lin_query.shape[1]
    device = lax.axis_index("ctx").astype(jnp.int32)
    block = device.reshape(1)

    heads = lax.axis_size("head")
    stacked = jnp.stack([soft_keys, soft_values])
    stacked, early = lax.optimization_barrier((stacked, projections))
    kv3, kv2, kv1 = (passed_along(stacked, offset) for offset in (3, 2, 1))
    proj = early.reshape(2, KV_HEADS, width, DH).transpose(1, 0, 2, 3)
    proj = lax.all_to_all(proj, "head", 0, 0, tiled=True)
    soft_query = pltpu.with_memory_space_constraint(soft_query, pltpu.HBM)
    soft_grad = pltpu.with_memory_space_constraint(soft_grad, pltpu.HBM)
    soft_dq, part3, part2, part1, own = softmax_call(
        block * length, doc_lengths.reshape(1, -1), soft_query, soft_grad, [kv3, kv2, kv1, stacked]
    )
    lin_query, own = lax.optimization_barrier((lin_query, own))
    lin_out, scaled, tail = forward_call(
        block, lin_query, lin_keys, lin_values, log_decay, state_in
    )
    summed = own
    for offset, part in ((3, part3), (2, part2), (1, part1)):
        summed = summed + passed_along(part, -offset).astype(F32)
    dkv, lin_out, proj = lax.optimization_barrier((summed.astype(BF16), lin_out, proj))
    soft_dk, soft_dv = dkv[:, :DH], dkv[:, DH:]

    same_core = [[2 * chip + core for chip in range(heads // 2)] for core in range(2)]
    copies = jnp.broadcast_to(dkv[None], (heads // 2,) + dkv.shape)
    own_dkv = lax.all_to_all(copies, "head", 0, 0, tiled=True, axis_index_groups=same_core)
    other_dkv = lax.ppermute(own_dkv, "head", [(i, i ^ 1) for i in range(heads)])
    core = (lax.axis_index("head").astype(jnp.int32) % 2).reshape(1)
    gated, stats = cotangent_call(
        core, own_dkv, other_dkv, proj, lin_grad, norm_gain.reshape(1, width), lin_out
    )
    stats = lax.all_to_all(stats, "head", 0, 0, tiled=True)
    dout, summary = dout_call(stats, gated, lin_out, scaled)
    weights = state_weights(log_decay, length, device)
    beside = near_far_call(block, lin_query, lin_keys, lin_values, dout, log_decay, state_in)
    after, (lin_dq, dk, dv) = after_states(summary, weights, beside)
    lin_dk, lin_dv = last_call(lin_keys, lin_values, dk, dv, tail, after)
    return (lin_dq, lin_dk, lin_dv, soft_dq, soft_dk, soft_dv)


def solution(mesh):
    in_specs = (
        P("ctx", "head"), P("ctx", "head"), P("ctx", "head"), P("ctx", "head"),
        P("head"), P("head", None), P("ctx", "head", None, None),
        P("ctx", "head"), P("ctx", "head"), P("ctx", "head"), P("ctx", "head"),
        P(None, None, "head"), P(),
    )
    out_specs = (P("ctx", "head"),) * 6
    return jax.shard_map(
        per_device, mesh=mesh, in_specs=in_specs, out_specs=out_specs, check_vma=False
    )
```

```python
import functools
import math

import jax
import jax.numpy as jnp
from jax import lax
from jax.experimental import pallas as pl
from jax.experimental.pallas import tpu as pltpu
from jax.sharding import PartitionSpec as P

DH = 128
Q_HEADS = 64
KV_HEADS = 8
GROUP = Q_HEADS // KV_HEADS
LIGHTNING_HEADS = 32
FEATURES = LIGHTNING_HEADS * DH
SUB = 4
QUAD = 4
AT_ONCE = 8
TILES = 2
epsilon = 1e-06

F32 = jnp.float32
BF16 = jnp.bfloat16
NT = (((1,), (1,)), ((), ()))
NN = (((1,), (0,)), ((), ()))
TN = (((0,), (0,)), ((), ()))
VMEM_LIMIT = 48 * 1024 * 1024


def mm(a, b, dims=NN):
    return lax.dot_general(a, b, dims, preferred_element_type=F32)


def iota2(shape, dim):
    return lax.broadcasted_iota(jnp.int32, shape, dim)


def to_column(row):
    n = row.shape[1]
    return jnp.sum(jnp.where(iota2((n, n), 0) == iota2((n, n), 1), row, 0.0), axis=1, keepdims=True)


def to_row(column):
    n = column.shape[0]
    return jnp.sum(jnp.where(iota2((n, n), 0) == iota2((n, n), 1), column, 0.0), axis=0, keepdims=True)


def decay_sums(log_row):
    n = log_row.shape[1]
    first, second = iota2((n, n), 0), iota2((n, n), 1)
    g_col = jnp.sum(jnp.where(second <= first, log_row, 0.0), axis=1, keepdims=True)
    return g_col, to_row(g_col)


def softmax_kernel(
    length, base_ref, lens_ref, q_ref, do_ref, kv3, kv2, kv1, kv0,
    dq_ref, part3, part2, part1, own, k_win, v_win, k_t, bias, acc_k, acc_v,
):
    tile, pair = pl.program_id(0), pl.program_id(1)
    first = jnp.logical_and(tile == 0, pair == 0)
    final = jnp.logical_and(tile == pl.num_programs(0) - 1, pair == pl.num_programs(1) - 1)
    rows = q_ref.shape[0]
    reach = bias.shape[0]
    scale = DH ** -0.5

    @pl.when(first)
    def _():
        for slot, kv in enumerate((kv3, kv2, kv1, kv0)):
            here = slice(slot * length, (slot + 1) * length)
            k_win[here, :] = kv[0]
            v_win[here, :] = kv[1]
            k_t[:, here] = kv[0].astype(F32).T.astype(BF16)
        acc_k[...] = jnp.zeros_like(acc_k)
        acc_v[...] = jnp.zeros_like(acc_v)

    @pl.when(pair == 0)
    def _():
        docs = lens_ref.shape[1]
        lens = jnp.where(iota2((docs, docs), 1) <= iota2((docs, docs), 0), lens_ref[...], 0)
        ends = jnp.sum(lens, axis=1, keepdims=True)
        base = base_ref[0] + tile * rows
        t_row = base + iota2((docs, rows), 1)
        start = jnp.max(jnp.where(ends <= t_row, ends, 0), axis=0, keepdims=True)
        s_pos = base - (SUB - 1) * length + iota2((reach, rows), 0)
        t_pos = base + iota2((reach, rows), 1)
        hidden = jnp.where((s_pos <= t_pos) & (s_pos >= start), 0.0, -1e30)
        for head in range(AT_ONCE):
            bias[:, head * rows:(head + 1) * rows] = hidden

    def stacked(ref):
        return jnp.concatenate([ref[:, h * DH:(h + 1) * DH] for h in range(AT_ONCE)], axis=0)

    window = pl.ds(pl.multiple_of(tile * rows, rows), reach)
    q = stacked(q_ref)
    do = stacked(do_ref)
    scores = mm(k_win[window, :], q, NT) * (scale * math.log2(math.e)) + bias[...]
    highest = jnp.max(scores, axis=0, keepdims=True)
    raised = jnp.exp2(scores - highest)
    inverse = 1.0 / jnp.sum(raised, axis=0, keepdims=True)
    grad_probs = mm(v_win[window, :], do, NT)
    delta = jnp.sum(raised * grad_probs, axis=0, keepdims=True) * inverse
    prob = raised * inverse
    dscore = (prob * (grad_probs - delta)).astype(BF16)
    acc_v[window, :] += mm(prob.astype(BF16), do)
    acc_k[window, :] += mm(dscore, q)
    dq = (mm(k_t[:, window], dscore) * scale).T
    for head in range(AT_ONCE):
        dq_ref[:, head * DH:(head + 1) * DH] = dq[head * rows:(head + 1) * rows, :].astype(BF16)

    @pl.when(final)
    def _():
        for slot, out in enumerate((part3, part2, part1, own)):
            here = slice(slot * length, (slot + 1) * length)
            out[:, :DH] = (acc_k[here, :] * scale).astype(out.dtype)
            out[:, DH:] = acc_v[here, :].astype(out.dtype)


def softmax_call(base, lens, q, do, windows):
    length = q.shape[0]
    rows = length // TILES
    whole = lambda *shape: pl.BlockSpec(shape, lambda i, j: (0,) * len(shape))
    per_pair = pl.BlockSpec((rows, AT_ONCE * DH), lambda i, j: (i, j))
    window = SUB * length
    reach = window - length + rows
    pair = jax.ShapeDtypeStruct((length, 2 * DH), BF16)
    return pl.pallas_call(
        functools.partial(softmax_kernel, length),
        out_shape=(
            jax.ShapeDtypeStruct(q.shape, BF16), pair, pair, pair,
            jax.ShapeDtypeStruct((length, 2 * DH), F32),
        ),
        grid=(TILES, GROUP // AT_ONCE),
        in_specs=[
            pl.BlockSpec(memory_space=pltpu.SMEM), whole(1, lens.shape[1]), per_pair, per_pair,
        ] + [whole(2, length, DH)] * SUB,
        out_specs=(per_pair,) + (whole(length, 2 * DH),) * SUB,
        scratch_shapes=[
            pltpu.VMEM((window, DH), BF16), pltpu.VMEM((window, DH), BF16),
            pltpu.VMEM((DH, window), BF16), pltpu.VMEM((reach, AT_ONCE * rows), F32),
            pltpu.VMEM((window, DH), F32), pltpu.VMEM((window, DH), F32),
        ],
        compiler_params=pltpu.CompilerParams(vmem_limit_bytes=VMEM_LIMIT),
        cost_estimate=pl.CostEstimate(
            flops=200 * GROUP * window * length * DH * 4, bytes_accessed=4 * 1024 * 1024,
            transcendentals=GROUP * window * length,
        ),
        name="softmax_backward",
    )(base, lens, q, do, *windows)


def forward_kernel(
    block_ref, q_ref, k_ref, v_ref, gain_ref, log_ref, state_ref, out_ref, gained_ref, scaled_ref, tail_ref
):
    head = pl.program_id(0)
    length = q_ref.shape[0]
    g_col, g_row = decay_sums(log_ref[pl.ds(head, 1), :])
    causal = iota2((length, length), 0) >= iota2((length, length), 1)
    weights = jnp.where(causal, jnp.exp(jnp.minimum(g_col - g_row, 0.0)), 0.0)
    near = (mm(q_ref[...], k_ref[...], NT) * weights).astype(BF16)
    scaled = (q_ref[...].astype(F32) * jnp.exp(g_col)).astype(BF16)
    out = (mm(near, v_ref[...]) + mm(scaled, state_ref[0, 0])) * (1.0 / DH)
    out_ref[...] = out
    gained_ref[...] = (out * gain_ref[...]).astype(BF16)
    scaled_ref[...] = scaled
    tail_ref[...] = jnp.broadcast_to(jnp.exp(g_col[length - 1:, :] - g_col), out.shape)


def per_head_spec(length):
    return pl.BlockSpec((length, DH), lambda h, b: (0, h))


def state_spec():
    return pl.BlockSpec((1, 1, DH, DH), lambda h, b: (0, h, 0, 0))


def log_spec(heads, length):
    return pl.BlockSpec((heads, length), lambda h, b: (0, b[0]))


def forward_call(block, q, k, v, gain, log_decay, state):
    length, heads = q.shape[0], q.shape[1] // DH
    wide = per_head_spec(length)
    like = lambda dtype: jax.ShapeDtypeStruct(q.shape, dtype)
    return pl.pallas_call(
        forward_kernel,
        out_shape=(like(F32), like(BF16), like(BF16), like(F32)),
        grid_spec=pltpu.PrefetchScalarGridSpec(
            num_scalar_prefetch=1, grid=(heads,),
            in_specs=[
                wide, wide, wide, pl.BlockSpec((1, DH), lambda h, b: (0, h)), log_spec(heads, length),
                state_spec(),
            ],
            out_specs=(wide, wide, wide, wide),
        ),
        cost_estimate=pl.CostEstimate(
            flops=heads * length * DH * (4 * length + 2 * DH) * 8, bytes_accessed=4 * 1024 * 1024,
            transcendentals=heads * length * length,
        ),
        name="lightning_forward",
    )(block, q, k, v, gain, log_decay, state)


def pack_kernel(proj_ref, packed_ref):
    packed_ref[:, :, :DH] = proj_ref[0]
    packed_ref[:, :, DH:] = proj_ref[1]


def pack_call(projections, chips):
    rows = projections.shape[1] // chips
    some = chips // 2
    return pl.pallas_call(
        pack_kernel,
        grid=(chips // some,),
        in_specs=[pl.BlockSpec((2, some, rows, DH), lambda i: (0, i, 0, 0))],
        out_specs=pl.BlockSpec((some, rows, 2 * DH), lambda i: (i, 0, 0)),
        out_shape=jax.ShapeDtypeStruct((chips, rows, 2 * DH), BF16),
        cost_estimate=pl.CostEstimate(flops=0, bytes_accessed=4 * 1024 * 1024, transcendentals=0),
        name="pack",
    )(projections.reshape(2, chips, rows, DH))


PARTS = 2


def cotangent_kernel(
    core_ref, dkv_ref, proj_ref, sibling_ref, grad_ref, gain_ref, out_ref,
    gated_ref, carried_ref, stats_ref, squares, cross,
):
    step = pl.program_id(0)
    carried = jnp.zeros(carried_ref.shape, F32)
    for chip in range(dkv_ref.shape[0]):
        carried += mm(dkv_ref[chip], proj_ref[chip], NT)

    @pl.when(step == 0)
    def _():
        squares[...] = jnp.zeros_like(squares)
        cross[...] = jnp.zeros_like(cross)

    @pl.when(step < PARTS)
    def _():
        carried_ref[...] = carried
        cross[...] += jnp.sum(sibling_ref[...].astype(F32) * carried, axis=1, keepdims=True)

    @pl.when(step >= PARTS)
    def _():
        gated = gain_ref[...] * (grad_ref[...].astype(F32) + carried)
        gated_ref[...] = gated
        out = out_ref[...]
        squares[...] += jnp.sum(out * out, axis=1, keepdims=True)
        cross[...] += jnp.sum(gated * out, axis=1, keepdims=True)

    @pl.when(step == pl.num_programs(0) - 1)
    def _():
        rows = iota2(stats_ref.shape[1:], 0)
        stats = jnp.where(
            rows == 0, to_row(squares[...]), jnp.where(rows == 1, to_row(cross[...]), 0.0)
        )
        for copy in range(stats_ref.shape[0]):
            stats_ref[copy] = stats


def cotangent_call(core, dkv, proj, sibling, grad, gain, out):
    length, width = grad.shape
    part = width // PARTS
    whole = lambda *shape: pl.BlockSpec(shape, lambda i, c: (0,) * len(shape))
    early = pl.BlockSpec((length, part), lambda i, c: (0, jnp.minimum(i, PARTS - 1)))
    late = pl.BlockSpec((length, part), lambda i, c: (0, jnp.maximum(i - PARTS, 0)))

    def features(i, c):
        side = jnp.where(i < PARTS, 1 - c[0], c[0])
        return (0, side * PARTS + i % PARTS, 0)

    return pl.pallas_call(
        cotangent_kernel,
        out_shape=(
            jax.ShapeDtypeStruct(grad.shape, F32), jax.ShapeDtypeStruct(grad.shape, F32),
            jax.ShapeDtypeStruct((KV_HEADS, 8, length), F32),
        ),
        grid_spec=pltpu.PrefetchScalarGridSpec(
            num_scalar_prefetch=1, grid=(2 * PARTS,),
            in_specs=[
                whole(*dkv.shape), pl.BlockSpec((dkv.shape[0], part, 2 * DH), features), early, late,
                pl.BlockSpec((1, part), lambda i, c: (0, jnp.maximum(i - PARTS, 0))), late,
            ],
            out_specs=(late, early, whole(KV_HEADS, 8, length)),
            scratch_shapes=[pltpu.VMEM((length, 1), F32), pltpu.VMEM((length, 1), F32)],
        ),
        compiler_params=pltpu.CompilerParams(vmem_limit_bytes=VMEM_LIMIT),
        name="cotangent",
    )(core, dkv, proj, sibling, grad, gain, out)


def dout_kernel(stats_ref, gated_ref, carried_ref, gain_ref, out_ref, scaled_ref, dout_ref, summary_ref):
    stats = stats_ref[0]
    for source in range(1, stats_ref.shape[0]):
        stats += stats_ref[source]
    inverse = 1.0 / jnp.sqrt(stats[0:1, :] * (1.0 / FEATURES) + epsilon)
    factor = stats[1:2, :] * (inverse * inverse * inverse) * (1.0 / FEATURES)
    gated = gated_ref[...] + gain_ref[...] * carried_ref[...]
    low = (gated * to_column(inverse) - out_ref[...] * to_column(factor)).astype(BF16)
    dout_ref[...] = low
    for head in range(summary_ref.shape[0]):
        columns = slice(head * DH, (head + 1) * DH)
        summary_ref[head] = mm(scaled_ref[:, columns], low[:, columns], TN).astype(BF16)


def dout_call(stats, gated, carried, gain, out, scaled):
    return pl.pallas_call(
        dout_kernel,
        out_shape=(
            jax.ShapeDtypeStruct(out.shape, BF16),
            jax.ShapeDtypeStruct((out.shape[1] // DH, DH, DH), BF16),
        ),
        name="dout_summary",
    )(stats, gated, carried, gain, out, scaled)


def near_far_kernel(
    block_ref, q_ref, k_ref, v_ref, dout_ref, log_ref, state_ref, dq_ref, dk_ref, dv_ref
):
    head = pl.program_id(0)
    length = q_ref.shape[0]
    g_col, g_row = decay_sums(log_ref[pl.ds(head, 1), :])
    first, second = iota2((length, length), 0), iota2((length, length), 1)
    gap = g_col - g_row
    weights = jnp.where(first >= second, jnp.exp(jnp.minimum(gap, 0.0)), 0.0)
    turned = jnp.where(second >= first, jnp.exp(jnp.minimum(-gap, 0.0)), 0.0)
    q, k, v, dout = q_ref[...], k_ref[...], v_ref[...], dout_ref[...]
    far = (mm(dout, v, NT) * weights).astype(BF16)
    far_turned = (mm(v, dout, NT) * turned).astype(BF16)
    near_turned = (mm(k, q, NT) * turned).astype(BF16)
    dq = mm(far, k) + jnp.exp(g_col) * mm(dout, state_ref[0, 0], NT)
    dq_ref[...] = (dq * (1.0 / DH)).astype(BF16)
    dk_ref[...] = mm(far_turned, q)
    dv_ref[...] = mm(near_turned, dout)


def near_far_call(block, q, k, v, dout, log_decay, state):
    length, heads = q.shape[0], q.shape[1] // DH
    wide = per_head_spec(length)
    return pl.pallas_call(
        near_far_kernel,
        out_shape=(
            jax.ShapeDtypeStruct(q.shape, BF16), jax.ShapeDtypeStruct(q.shape, F32),
            jax.ShapeDtypeStruct(q.shape, F32),
        ),
        grid_spec=pltpu.PrefetchScalarGridSpec(
            num_scalar_prefetch=1, grid=(heads,),
            in_specs=[wide, wide, wide, wide, log_spec(heads, length), state_spec()],
            out_specs=(wide, wide, wide),
        ),
        cost_estimate=pl.CostEstimate(
            flops=heads * length * DH * (12 * length + 2 * DH) * 8, bytes_accessed=4 * 1024 * 1024,
            transcendentals=2 * heads * length * length,
        ),
        name="near_far",
    )(block, q, k, v, dout, log_decay, state)


def last_kernel(k_ref, v_ref, dk_ref, dv_ref, tail_ref, after_ref, dk_out, dv_out):
    for head in range(after_ref.shape[0]):
        at = slice(head * DH, (head + 1) * DH)
        tail = tail_ref[:, at]
        after = after_ref[head]
        dk = dk_ref[:, at] + tail * mm(v_ref[:, at], after, NT)
        dv = dv_ref[:, at] + tail * mm(k_ref[:, at], after)
        dk_out[:, at] = (dk * (1.0 / DH)).astype(BF16)
        dv_out[:, at] = (dv * (1.0 / DH)).astype(BF16)


def last_call(k, v, dk, dv, tail, after):
    return pl.pallas_call(
        last_kernel,
        out_shape=(jax.ShapeDtypeStruct(k.shape, BF16), jax.ShapeDtypeStruct(k.shape, BF16)),
        name="last",
    )(k, v, dk, dv, tail, after)


ENTER, LEAVE, INNER, CARRY = 0, 16, 32, 96


def state_weights(log_decay, length, device):
    square = QUAD * QUAD
    group, row = device // QUAD % QUAD, device // square
    decays = lax.dynamic_slice_in_dim(log_decay, row, 1, 0)
    gamma = jnp.sum(decays.reshape(-1, length), axis=1)
    block = jnp.arange(gamma.shape[0], dtype=jnp.int32)
    quad = jnp.arange(QUAD, dtype=jnp.int32)
    first = quad * square + group * QUAD
    own = (first[:, None] + quad[None, :]).reshape(-1)
    every = jnp.arange(square, dtype=jnp.int32) * QUAD
    low = jnp.concatenate(
        [jnp.repeat(first - 1, QUAD), own, jnp.repeat(own, QUAD), jnp.repeat(first + QUAD - 1, square)]
    )
    high = jnp.concatenate(
        [own, jnp.repeat(first + QUAD, QUAD), jnp.tile(own.reshape(QUAD, QUAD), (1, QUAD)).reshape(-1),
         jnp.tile(every, QUAD)]
    )
    inside = (block[None, :] > low[:, None]) & (block[None, :] < high[:, None])
    factors = jnp.exp(jnp.sum(jnp.where(inside, gamma[None, :], 0.0), axis=1))
    return jnp.where(high > low, factors, 0.0)


def rise_kernel(weight_ref, blocks_ref, total_ref):
    for row in range(QUAD):
        total = jnp.zeros(blocks_ref.shape[1:], F32)
        for z in range(QUAD):
            at = row * QUAD + z
            total += weight_ref[ENTER + at] * blocks_ref[at].astype(F32)
        total = total.astype(BF16)
        for copy in range(QUAD):
            total_ref[copy, row] = total


def after_kernel(weight_ref, blocks_ref, totals_ref, after_ref):
    square = QUAD * QUAD
    for row in range(QUAD):
        carry = jnp.zeros(blocks_ref.shape[1:], F32)
        for g in range(square):
            carry += weight_ref[CARRY + row * square + g] * totals_ref[g % QUAD, g // QUAD].astype(F32)
        for z in range(QUAD):
            at = row * QUAD + z
            after = weight_ref[LEAVE + at] * carry
            for later in range(z + 1, QUAD):
                after += weight_ref[INNER + at * QUAD + later] * blocks_ref[row * QUAD + later].astype(F32)
            after_ref[at] = after.astype(BF16)


def after_states(summary, weights, beside):
    square = QUAD * QUAD
    rows = lax.axis_size("ctx") // square
    near = [
        [r * square + g * QUAD + z for r in range(rows) for z in range(QUAD)] for g in range(QUAD)
    ]
    far = [[r * square + g * QUAD + z for g in range(QUAD)] for r in range(rows) for z in range(QUAD)]
    smem = pl.BlockSpec(memory_space=pltpu.SMEM)
    vmem = pl.BlockSpec(memory_space=pltpu.VMEM)
    swap = lambda x, groups: lax.all_to_all(x, "ctx", 0, 0, tiled=True, axis_index_groups=groups)
    part = summary.size // square // DH
    blocks = swap(summary.reshape(square, part, DH), near)
    totals = pl.pallas_call(
        rise_kernel, out_shape=jax.ShapeDtypeStruct((QUAD, rows, part, DH), BF16),
        in_specs=[smem, vmem], out_specs=vmem, name="rise",
    )(weights, blocks)
    totals, beside = lax.optimization_barrier((swap(totals, far), beside))
    after = pl.pallas_call(
        after_kernel, out_shape=jax.ShapeDtypeStruct(blocks.shape, BF16),
        in_specs=[smem, vmem, vmem], out_specs=vmem, name="after_states",
    )(weights, blocks, totals)
    return swap(after, near).reshape(summary.shape), beside


def passed_along(block, distance):
    devices = range(lax.axis_size("ctx"))
    route = [(i - distance, i) for i in devices if i - distance in devices]
    return lax.ppermute(block, "ctx", route)


def per_device(
    lin_query, lin_keys, lin_values, lin_grad, norm_gain, log_decay, state_in,
    soft_query, soft_keys, soft_values, soft_grad, projections, doc_lengths,
):
    length = lin_query.shape[0]
    width = lin_query.shape[1]
    device = lax.axis_index("ctx").astype(jnp.int32)
    block = device.reshape(1)

    heads = lax.axis_size("head")
    chips = heads // 2
    same_core = [[2 * chip + core for chip in range(chips)] for core in range(2)]
    sibling = [(i, i ^ 1) for i in range(heads)]
    core = (lax.axis_index("head").astype(jnp.int32) % 2).reshape(1)
    gain = norm_gain.reshape(1, width)

    stacked = jnp.stack([soft_keys, soft_values])
    stacked, early = lax.optimization_barrier((stacked, projections))
    kv3, kv2, kv1 = (passed_along(stacked, offset) for offset in (3, 2, 1))
    proj = lax.all_to_all(
        pack_call(early, chips), "head", 0, 0, tiled=True, axis_index_groups=same_core
    )
    soft_query = pltpu.with_memory_space_constraint(soft_query, pltpu.HBM)
    soft_grad = pltpu.with_memory_space_constraint(soft_grad, pltpu.HBM)
    soft_dq, part3, part2, part1, own = softmax_call(
        block * length, doc_lengths.reshape(1, -1), soft_query, soft_grad, [kv3, kv2, kv1, stacked]
    )
    lin_query, own = lax.optimization_barrier((lin_query, own))
    lin_out, gained, scaled, tail = forward_call(
        block, lin_query, lin_keys, lin_values, gain, log_decay, state_in
    )
    gained = lax.ppermute(gained, "head", sibling)
    summed = own
    for offset, part in ((3, part3), (2, part2), (1, part1)):
        summed = summed + passed_along(part, -offset).astype(F32)
    dkv, lin_out, gained, proj, late_decay = lax.optimization_barrier(
        (summed.astype(BF16), lin_out, gained, proj, log_decay)
    )
    weights = state_weights(late_decay, length, device)
    soft_dk, soft_dv = dkv[:, :DH], dkv[:, DH:]

    copies = jnp.broadcast_to(dkv[None], (chips,) + dkv.shape)
    dkv_all = lax.all_to_all(copies, "head", 0, 0, tiled=True, axis_index_groups=same_core)
    gated, carried, stats = cotangent_call(core, dkv_all, proj, gained, lin_grad, gain, lin_out)
    carried = lax.ppermute(carried, "head", sibling)
    stats = lax.all_to_all(stats, "head", 0, 0, tiled=True)
    dout, summary = dout_call(stats, gated, carried, gain, lin_out, scaled)
    beside = near_far_call(block, lin_query, lin_keys, lin_values, dout, log_decay, state_in)
    after, (lin_dq, dk, dv) = after_states(summary, weights, beside)
    lin_dk, lin_dv = last_call(lin_keys, lin_values, dk, dv, tail, after)
    return (lin_dq, lin_dk, lin_dv, soft_dq, soft_dk, soft_dv)


def solution(mesh):
    in_specs = (
        P("ctx", "head"), P("ctx", "head"), P("ctx", "head"), P("ctx", "head"),
        P("head"), P("head", None), P("ctx", "head", None, None),
        P("ctx", "head"), P("ctx", "head"), P("ctx", "head"), P("ctx", "head"),
        P(None, None, "head"), P(),
    )
    out_specs = (P("ctx", "head"),) * 6
    return jax.shard_map(
        per_device, mesh=mesh, in_specs=in_specs, out_specs=out_specs, check_vma=False
    )
```

```python
import functools
import math

import jax
import jax.numpy as jnp
from jax import lax
from jax.experimental import pallas as pl
from jax.experimental.pallas import tpu as pltpu
from jax.sharding import PartitionSpec as P

DH = 128
Q_HEADS = 64
KV_HEADS = 8
GROUP = Q_HEADS // KV_HEADS
LIGHTNING_HEADS = 32
FEATURES = LIGHTNING_HEADS * DH
SUB = 4
QUAD = 4
AT_ONCE = 8
TILES = 2
epsilon = 1e-06

F32 = jnp.float32
BF16 = jnp.bfloat16
NT = (((1,), (1,)), ((), ()))
NN = (((1,), (0,)), ((), ()))
TN = (((0,), (0,)), ((), ()))
VMEM_LIMIT = 48 * 1024 * 1024


def mm(a, b, dims=NN):
    return lax.dot_general(a, b, dims, preferred_element_type=F32)


def iota2(shape, dim):
    return lax.broadcasted_iota(jnp.int32, shape, dim)


def to_column(row):
    n = row.shape[1]
    return jnp.sum(jnp.where(iota2((n, n), 0) == iota2((n, n), 1), row, 0.0), axis=1, keepdims=True)


def to_row(column):
    n = column.shape[0]
    return jnp.sum(jnp.where(iota2((n, n), 0) == iota2((n, n), 1), column, 0.0), axis=0, keepdims=True)


def decay_sums(log_row):
    n = log_row.shape[1]
    first, second = iota2((n, n), 0), iota2((n, n), 1)
    g_col = jnp.sum(jnp.where(second <= first, log_row, 0.0), axis=1, keepdims=True)
    return g_col, to_row(g_col)


def softmax_kernel(
    length, base_ref, lens_ref, q_ref, do_ref, kv3, kv2, kv1, kv0,
    dq_ref, part3, part2, part1, own, k_win, v_win, k_t, bias, acc_k, acc_v,
):
    tile, pair = pl.program_id(0), pl.program_id(1)
    first = jnp.logical_and(tile == 0, pair == 0)
    final = jnp.logical_and(tile == pl.num_programs(0) - 1, pair == pl.num_programs(1) - 1)
    rows = q_ref.shape[0]
    reach = bias.shape[0]
    scale = DH ** -0.5

    @pl.when(first)
    def _():
        for slot, kv in enumerate((kv3, kv2, kv1, kv0)):
            here = slice(slot * length, (slot + 1) * length)
            k_win[here, :] = kv[0]
            v_win[here, :] = kv[1]
            k_t[:, here] = kv[0].astype(F32).T.astype(BF16)
        acc_k[...] = jnp.zeros_like(acc_k)
        acc_v[...] = jnp.zeros_like(acc_v)

    @pl.when(pair == 0)
    def _():
        docs = lens_ref.shape[1]
        lens = jnp.where(iota2((docs, docs), 1) <= iota2((docs, docs), 0), lens_ref[...], 0)
        ends = jnp.sum(lens, axis=1, keepdims=True)
        base = base_ref[0] + tile * rows
        t_row = base + iota2((docs, rows), 1)
        start = jnp.max(jnp.where(ends <= t_row, ends, 0), axis=0, keepdims=True)
        s_pos = base - (SUB - 1) * length + iota2((reach, rows), 0)
        t_pos = base + iota2((reach, rows), 1)
        hidden = jnp.where((s_pos <= t_pos) & (s_pos >= start), 0.0, -1e30)
        for head in range(AT_ONCE):
            bias[:, head * rows:(head + 1) * rows] = hidden

    def stacked(ref):
        return jnp.concatenate([ref[:, h * DH:(h + 1) * DH] for h in range(AT_ONCE)], axis=0)

    window = pl.ds(pl.multiple_of(tile * rows, rows), reach)
    q = stacked(q_ref)
    do = stacked(do_ref)
    scores = mm(k_win[window, :], q, NT) * (scale * math.log2(math.e)) + bias[...]
    highest = jnp.max(scores, axis=0, keepdims=True)
    raised = jnp.exp2(scores - highest)
    inverse = 1.0 / jnp.sum(raised, axis=0, keepdims=True)
    grad_probs = mm(v_win[window, :], do, NT)
    delta = jnp.sum(raised * grad_probs, axis=0, keepdims=True) * inverse
    prob = raised * inverse
    dscore = (prob * (grad_probs - delta)).astype(BF16)
    acc_v[window, :] += mm(prob.astype(BF16), do)
    acc_k[window, :] += mm(dscore, q)
    dq = (mm(k_t[:, window], dscore) * scale).T
    for head in range(AT_ONCE):
        dq_ref[:, head * DH:(head + 1) * DH] = dq[head * rows:(head + 1) * rows, :].astype(BF16)

    @pl.when(final)
    def _():
        for slot, out in enumerate((part3, part2, part1, own)):
            here = slice(slot * length, (slot + 1) * length)
            out[:, :DH] = (acc_k[here, :] * scale).astype(out.dtype)
            out[:, DH:] = acc_v[here, :].astype(out.dtype)


def softmax_call(base, lens, q, do, windows):
    length = q.shape[0]
    rows = length // TILES
    whole = lambda *shape: pl.BlockSpec(shape, lambda i, j: (0,) * len(shape))
    per_pair = pl.BlockSpec((rows, AT_ONCE * DH), lambda i, j: (i, j))
    window = SUB * length
    reach = window - length + rows
    pair = jax.ShapeDtypeStruct((length, 2 * DH), BF16)
    return pl.pallas_call(
        functools.partial(softmax_kernel, length),
        out_shape=(
            jax.ShapeDtypeStruct(q.shape, BF16), pair, pair, pair,
            jax.ShapeDtypeStruct((length, 2 * DH), F32),
        ),
        grid=(TILES, GROUP // AT_ONCE),
        in_specs=[
            pl.BlockSpec(memory_space=pltpu.SMEM), whole(1, lens.shape[1]), per_pair, per_pair,
        ] + [whole(2, length, DH)] * SUB,
        out_specs=(per_pair,) + (whole(length, 2 * DH),) * SUB,
        scratch_shapes=[
            pltpu.VMEM((window, DH), BF16), pltpu.VMEM((window, DH), BF16),
            pltpu.VMEM((DH, window), BF16), pltpu.VMEM((reach, AT_ONCE * rows), F32),
            pltpu.VMEM((window, DH), F32), pltpu.VMEM((window, DH), F32),
        ],
        compiler_params=pltpu.CompilerParams(vmem_limit_bytes=VMEM_LIMIT),
        cost_estimate=pl.CostEstimate(
            flops=200 * GROUP * window * length * DH * 4, bytes_accessed=4 * 1024 * 1024,
            transcendentals=GROUP * window * length,
        ),
        name="softmax_backward",
    )(base, lens, q, do, *windows)


def forward_kernel(
    block_ref, q_ref, k_ref, v_ref, gain_ref, log_ref, state_ref, out_ref, gained_ref, scaled_ref, tail_ref
):
    head = pl.program_id(0)
    length = q_ref.shape[0]
    g_col, g_row = decay_sums(log_ref[pl.ds(head, 1), :])
    causal = iota2((length, length), 0) >= iota2((length, length), 1)
    weights = jnp.where(causal, jnp.exp(jnp.minimum(g_col - g_row, 0.0)), 0.0)
    near = (mm(q_ref[...], k_ref[...], NT) * weights).astype(BF16)
    scaled = (q_ref[...].astype(F32) * jnp.exp(g_col)).astype(BF16)
    out = (mm(near, v_ref[...]) + mm(scaled, state_ref[0, 0])) * (1.0 / DH)
    out_ref[...] = out
    gained_ref[...] = (out * gain_ref[...]).astype(BF16)
    scaled_ref[...] = scaled
    tail_ref[...] = jnp.broadcast_to(jnp.exp(g_col[length - 1:, :] - g_col), out.shape)


def per_head_spec(length):
    return pl.BlockSpec((length, DH), lambda h, b: (0, h))


def state_spec():
    return pl.BlockSpec((1, 1, DH, DH), lambda h, b: (0, h, 0, 0))


def log_spec(heads, length):
    return pl.BlockSpec((heads, length), lambda h, b: (0, b[0]))


def forward_call(block, q, k, v, gain, log_decay, state):
    length, heads = q.shape[0], q.shape[1] // DH
    wide = per_head_spec(length)
    like = lambda dtype: jax.ShapeDtypeStruct(q.shape, dtype)
    return pl.pallas_call(
        forward_kernel,
        out_shape=(like(F32), like(BF16), like(BF16), like(F32)),
        grid_spec=pltpu.PrefetchScalarGridSpec(
            num_scalar_prefetch=1, grid=(heads,),
            in_specs=[
                wide, wide, wide, pl.BlockSpec((1, DH), lambda h, b: (0, h)), log_spec(heads, length),
                state_spec(),
            ],
            out_specs=(wide, wide, wide, wide),
        ),
        cost_estimate=pl.CostEstimate(
            flops=heads * length * DH * (4 * length + 2 * DH) * 8, bytes_accessed=4 * 1024 * 1024,
            transcendentals=heads * length * length,
        ),
        name="lightning_forward",
    )(block, q, k, v, gain, log_decay, state)


def pack_kernel(proj_ref, packed_ref):
    packed_ref[:, :, :DH] = proj_ref[0]
    packed_ref[:, :, DH:] = proj_ref[1]


def pack_call(projections, chips):
    rows = projections.shape[1] // chips
    some = chips // 2
    return pl.pallas_call(
        pack_kernel,
        grid=(chips // some,),
        in_specs=[pl.BlockSpec((2, some, rows, DH), lambda i: (0, i, 0, 0))],
        out_specs=pl.BlockSpec((some, rows, 2 * DH), lambda i: (i, 0, 0)),
        out_shape=jax.ShapeDtypeStruct((chips, rows, 2 * DH), BF16),
        cost_estimate=pl.CostEstimate(flops=0, bytes_accessed=4 * 1024 * 1024, transcendentals=0),
        name="pack",
    )(projections.reshape(2, chips, rows, DH))


PARTS = 1


def cotangent_kernel(
    core_ref, dkv_ref, proj_ref, sibling_ref, grad_ref, gain_ref, out_ref,
    gated_ref, carried_ref, stats_ref, squares, cross,
):
    step = pl.program_id(0)
    carried = jnp.zeros(carried_ref.shape, F32)
    for chip in range(dkv_ref.shape[0]):
        carried += mm(dkv_ref[chip], proj_ref[chip], NT)

    @pl.when(step == 0)
    def _():
        squares[...] = jnp.zeros_like(squares)
        cross[...] = jnp.zeros_like(cross)

    @pl.when(step < PARTS)
    def _():
        carried_ref[...] = carried
        cross[...] += jnp.sum(sibling_ref[...].astype(F32) * carried, axis=1, keepdims=True)

    @pl.when(step >= PARTS)
    def _():
        gated = gain_ref[...] * (grad_ref[...].astype(F32) + carried)
        gated_ref[...] = gated
        out = out_ref[...]
        squares[...] += jnp.sum(out * out, axis=1, keepdims=True)
        cross[...] += jnp.sum(gated * out, axis=1, keepdims=True)

    @pl.when(step == pl.num_programs(0) - 1)
    def _():
        rows = iota2(stats_ref.shape[1:], 0)
        stats = jnp.where(
            rows == 0, to_row(squares[...]), jnp.where(rows == 1, to_row(cross[...]), 0.0)
        )
        for copy in range(stats_ref.shape[0]):
            stats_ref[copy] = stats


def cotangent_call(core, dkv, proj, sibling, grad, gain, out):
    length, width = grad.shape
    part = width // PARTS
    whole = lambda *shape: pl.BlockSpec(shape, lambda i, c: (0,) * len(shape))
    early = pl.BlockSpec((length, part), lambda i, c: (0, jnp.minimum(i, PARTS - 1)))
    late = pl.BlockSpec((length, part), lambda i, c: (0, jnp.maximum(i - PARTS, 0)))

    def features(i, c):
        side = jnp.where(i < PARTS, 1 - c[0], c[0])
        return (0, side * PARTS + i % PARTS, 0)

    return pl.pallas_call(
        cotangent_kernel,
        out_shape=(
            jax.ShapeDtypeStruct(grad.shape, F32), jax.ShapeDtypeStruct(grad.shape, F32),
            jax.ShapeDtypeStruct((KV_HEADS, 8, length), F32),
        ),
        grid_spec=pltpu.PrefetchScalarGridSpec(
            num_scalar_prefetch=1, grid=(2 * PARTS,),
            in_specs=[
                whole(*dkv.shape), pl.BlockSpec((dkv.shape[0], part, 2 * DH), features), early, late,
                pl.BlockSpec((1, part), lambda i, c: (0, jnp.maximum(i - PARTS, 0))), late,
            ],
            out_specs=(late, early, whole(KV_HEADS, 8, length)),
            scratch_shapes=[pltpu.VMEM((length, 1), F32), pltpu.VMEM((length, 1), F32)],
        ),
        compiler_params=pltpu.CompilerParams(vmem_limit_bytes=VMEM_LIMIT),
        name="cotangent",
    )(core, dkv, proj, sibling, grad, gain, out)


def dout_kernel(stats_ref, gated_ref, carried_ref, gain_ref, out_ref, scaled_ref, dout_ref, summary_ref):
    stats = stats_ref[0]
    for source in range(1, stats_ref.shape[0]):
        stats += stats_ref[source]
    inverse = 1.0 / jnp.sqrt(stats[0:1, :] * (1.0 / FEATURES) + epsilon)
    factor = stats[1:2, :] * (inverse * inverse * inverse) * (1.0 / FEATURES)
    gated = gated_ref[...] + gain_ref[...] * carried_ref[...]
    low = (gated * to_column(inverse) - out_ref[...] * to_column(factor)).astype(BF16)
    dout_ref[...] = low
    for head in range(summary_ref.shape[0]):
        columns = slice(head * DH, (head + 1) * DH)
        summary_ref[head] = mm(scaled_ref[:, columns], low[:, columns], TN).astype(BF16)


def dout_call(stats, gated, carried, gain, out, scaled):
    return pl.pallas_call(
        dout_kernel,
        out_shape=(
            jax.ShapeDtypeStruct(out.shape, BF16),
            jax.ShapeDtypeStruct((out.shape[1] // DH, DH, DH), BF16),
        ),
        name="dout_summary",
    )(stats, gated, carried, gain, out, scaled)


def near_far_kernel(
    block_ref, q_ref, k_ref, v_ref, dout_ref, log_ref, state_ref, dq_ref, dk_ref, dv_ref
):
    head = pl.program_id(0)
    length = q_ref.shape[0]
    g_col, g_row = decay_sums(log_ref[pl.ds(head, 1), :])
    first, second = iota2((length, length), 0), iota2((length, length), 1)
    gap = g_col - g_row
    weights = jnp.where(first >= second, jnp.exp(jnp.minimum(gap, 0.0)), 0.0)
    turned = jnp.where(second >= first, jnp.exp(jnp.minimum(-gap, 0.0)), 0.0)
    q, k, v, dout = q_ref[...], k_ref[...], v_ref[...], dout_ref[...]
    far = (mm(dout, v, NT) * weights).astype(BF16)
    far_turned = (mm(v, dout, NT) * turned).astype(BF16)
    near_turned = (mm(k, q, NT) * turned).astype(BF16)
    dq = mm(far, k) + jnp.exp(g_col) * mm(dout, state_ref[0, 0], NT)
    dq_ref[...] = (dq * (1.0 / DH)).astype(BF16)
    dk_ref[...] = mm(far_turned, q)
    dv_ref[...] = mm(near_turned, dout)


def near_far_call(block, q, k, v, dout, log_decay, state):
    length, heads = q.shape[0], q.shape[1] // DH
    wide = per_head_spec(length)
    return pl.pallas_call(
        near_far_kernel,
        out_shape=(
            jax.ShapeDtypeStruct(q.shape, BF16), jax.ShapeDtypeStruct(q.shape, F32),
            jax.ShapeDtypeStruct(q.shape, F32),
        ),
        grid_spec=pltpu.PrefetchScalarGridSpec(
            num_scalar_prefetch=1, grid=(heads,),
            in_specs=[wide, wide, wide, wide, log_spec(heads, length), state_spec()],
            out_specs=(wide, wide, wide),
        ),
        cost_estimate=pl.CostEstimate(
            flops=heads * length * DH * (12 * length + 2 * DH) * 8, bytes_accessed=4 * 1024 * 1024,
            transcendentals=2 * heads * length * length,
        ),
        name="near_far",
    )(block, q, k, v, dout, log_decay, state)


def last_kernel(k_ref, v_ref, dk_ref, dv_ref, tail_ref, after_ref, dk_out, dv_out):
    for head in range(after_ref.shape[0]):
        at = slice(head * DH, (head + 1) * DH)
        tail = tail_ref[:, at]
        after = after_ref[head]
        dk = dk_ref[:, at] + tail * mm(v_ref[:, at], after, NT)
        dv = dv_ref[:, at] + tail * mm(k_ref[:, at], after)
        dk_out[:, at] = (dk * (1.0 / DH)).astype(BF16)
        dv_out[:, at] = (dv * (1.0 / DH)).astype(BF16)


def last_call(k, v, dk, dv, tail, after):
    return pl.pallas_call(
        last_kernel,
        out_shape=(jax.ShapeDtypeStruct(k.shape, BF16), jax.ShapeDtypeStruct(k.shape, BF16)),
        name="last",
    )(k, v, dk, dv, tail, after)


ENTER, LEAVE, INNER, CARRY = 0, 16, 32, 96


def state_weights(log_decay, length, device):
    square = QUAD * QUAD
    group, row = device // QUAD % QUAD, device // square
    decays = lax.dynamic_slice_in_dim(log_decay, row, 1, 0)
    gamma = jnp.sum(decays.reshape(-1, length), axis=1)
    block = jnp.arange(gamma.shape[0], dtype=jnp.int32)
    quad = jnp.arange(QUAD, dtype=jnp.int32)
    first = quad * square + group * QUAD
    own = (first[:, None] + quad[None, :]).reshape(-1)
    every = jnp.arange(square, dtype=jnp.int32) * QUAD
    low = jnp.concatenate(
        [jnp.repeat(first - 1, QUAD), own, jnp.repeat(own, QUAD), jnp.repeat(first + QUAD - 1, square)]
    )
    high = jnp.concatenate(
        [own, jnp.repeat(first + QUAD, QUAD), jnp.tile(own.reshape(QUAD, QUAD), (1, QUAD)).reshape(-1),
         jnp.tile(every, QUAD)]
    )
    inside = (block[None, :] > low[:, None]) & (block[None, :] < high[:, None])
    factors = jnp.exp(jnp.sum(jnp.where(inside, gamma[None, :], 0.0), axis=1))
    return jnp.where(high > low, factors, 0.0)


def rise_kernel(weight_ref, blocks_ref, total_ref):
    for row in range(QUAD):
        total = jnp.zeros(blocks_ref.shape[1:], F32)
        for z in range(QUAD):
            at = row * QUAD + z
            total += weight_ref[ENTER + at] * blocks_ref[at].astype(F32)
        total = total.astype(BF16)
        for copy in range(QUAD):
            total_ref[copy, row] = total


def after_kernel(weight_ref, blocks_ref, totals_ref, after_ref):
    square = QUAD * QUAD
    for row in range(QUAD):
        carry = jnp.zeros(blocks_ref.shape[1:], F32)
        for g in range(square):
            carry += weight_ref[CARRY + row * square + g] * totals_ref[g % QUAD, g // QUAD].astype(F32)
        for z in range(QUAD):
            at = row * QUAD + z
            after = weight_ref[LEAVE + at] * carry
            for later in range(z + 1, QUAD):
                after += weight_ref[INNER + at * QUAD + later] * blocks_ref[row * QUAD + later].astype(F32)
            after_ref[at] = after.astype(BF16)


def after_states(summary, weights, beside):
    square = QUAD * QUAD
    rows = lax.axis_size("ctx") // square
    near = [
        [r * square + g * QUAD + z for r in range(rows) for z in range(QUAD)] for g in range(QUAD)
    ]
    far = [[r * square + g * QUAD + z for g in range(QUAD)] for r in range(rows) for z in range(QUAD)]
    smem = pl.BlockSpec(memory_space=pltpu.SMEM)
    vmem = pl.BlockSpec(memory_space=pltpu.VMEM)
    swap = lambda x, groups: lax.all_to_all(x, "ctx", 0, 0, tiled=True, axis_index_groups=groups)
    part = summary.size // square // DH
    blocks = swap(summary.reshape(square, part, DH), near)
    totals = pl.pallas_call(
        rise_kernel, out_shape=jax.ShapeDtypeStruct((QUAD, rows, part, DH), BF16),
        in_specs=[smem, vmem], out_specs=vmem, name="rise",
    )(weights, blocks)
    totals, beside = lax.optimization_barrier((swap(totals, far), beside))
    after = pl.pallas_call(
        after_kernel, out_shape=jax.ShapeDtypeStruct(blocks.shape, BF16),
        in_specs=[smem, vmem, vmem], out_specs=vmem, name="after_states",
    )(weights, blocks, totals)
    return swap(after, near).reshape(summary.shape), beside


def passed_along(block, distance):
    devices = range(lax.axis_size("ctx"))
    route = [(i - distance, i) for i in devices if i - distance in devices]
    return lax.ppermute(block, "ctx", route)


def per_device(
    lin_query, lin_keys, lin_values, lin_grad, norm_gain, log_decay, state_in,
    soft_query, soft_keys, soft_values, soft_grad, projections, doc_lengths,
):
    length = lin_query.shape[0]
    width = lin_query.shape[1]
    device = lax.axis_index("ctx").astype(jnp.int32)
    block = device.reshape(1)

    heads = lax.axis_size("head")
    chips = heads // 2
    same_core = [[2 * chip + core for chip in range(chips)] for core in range(2)]
    sibling = [(i, i ^ 1) for i in range(heads)]
    core = (lax.axis_index("head").astype(jnp.int32) % 2).reshape(1)
    gain = norm_gain.reshape(1, width)

    stacked = jnp.stack([soft_keys, soft_values])
    stacked, early = lax.optimization_barrier((stacked, projections))
    kv2, kv1 = (passed_along(stacked, offset) for offset in (2, 1))
    kv2, packed = lax.optimization_barrier((kv2, pack_call(early, chips)))
    kv3 = passed_along(kv2, 1)
    proj = lax.all_to_all(
        packed, "head", 0, 0, tiled=True, axis_index_groups=same_core
    )
    soft_query = pltpu.with_memory_space_constraint(soft_query, pltpu.HBM)
    soft_grad = pltpu.with_memory_space_constraint(soft_grad, pltpu.HBM)
    soft_dq, part3, part2, part1, own = softmax_call(
        block * length, doc_lengths.reshape(1, -1), soft_query, soft_grad, [kv3, kv2, kv1, stacked]
    )
    lin_query, own = lax.optimization_barrier((lin_query, own))
    lin_out, gained, scaled, tail = forward_call(
        block, lin_query, lin_keys, lin_values, gain, log_decay, state_in
    )
    gained = lax.ppermute(gained, "head", sibling)
    summed = own
    for offset, part in ((3, part3), (2, part2), (1, part1)):
        summed = summed + passed_along(part, -offset).astype(F32)
    dkv = summed.astype(BF16)
    copies, lin_out, gained, proj, late_decay = lax.optimization_barrier(
        (jnp.broadcast_to(dkv[None], (chips,) + dkv.shape), lin_out, gained, proj, log_decay)
    )
    weights = state_weights(late_decay, length, device)
    soft_dk, soft_dv = dkv[:, :DH], dkv[:, DH:]

    dkv_all = lax.all_to_all(copies, "head", 0, 0, tiled=True, axis_index_groups=same_core)
    gated, carried, stats = cotangent_call(core, dkv_all, proj, gained, lin_grad, gain, lin_out)
    carried = lax.ppermute(carried, "head", sibling)
    stats = lax.all_to_all(stats, "head", 0, 0, tiled=True)
    dout, summary = dout_call(stats, gated, carried, gain, lin_out, scaled)
    beside = near_far_call(block, lin_query, lin_keys, lin_values, dout, log_decay, state_in)
    after, (lin_dq, dk, dv) = after_states(summary, weights, beside)
    lin_dk, lin_dv = last_call(lin_keys, lin_values, dk, dv, tail, after)
    return (lin_dq, lin_dk, lin_dv, soft_dq, soft_dk, soft_dv)


def solution(mesh):
    in_specs = (
        P("ctx", "head"), P("ctx", "head"), P("ctx", "head"), P("ctx", "head"),
        P("head"), P("head", None), P("ctx", "head", None, None),
        P("ctx", "head"), P("ctx", "head"), P("ctx", "head"), P("ctx", "head"),
        P(None, None, "head"), P(),
    )
    out_specs = (P("ctx", "head"),) * 6
    return jax.shard_map(
        per_device, mesh=mesh, in_specs=in_specs, out_specs=out_specs, check_vma=False
    )
```

```python
import functools
import math

import jax
import jax.numpy as jnp
from jax import lax
from jax.experimental import pallas as pl
from jax.experimental.pallas import tpu as pltpu
from jax.sharding import PartitionSpec as P

DH = 128
Q_HEADS = 64
KV_HEADS = 8
GROUP = Q_HEADS // KV_HEADS
LIGHTNING_HEADS = 32
FEATURES = LIGHTNING_HEADS * DH
SUB = 4
QUAD = 4
AT_ONCE = 8
TILES = 2
epsilon = 1e-06

F32 = jnp.float32
BF16 = jnp.bfloat16
NT = (((1,), (1,)), ((), ()))
NN = (((1,), (0,)), ((), ()))
TN = (((0,), (0,)), ((), ()))
VMEM_LIMIT = 48 * 1024 * 1024


def mm(a, b, dims=NN):
    return lax.dot_general(a, b, dims, preferred_element_type=F32)


def iota2(shape, dim):
    return lax.broadcasted_iota(jnp.int32, shape, dim)


def to_column(row):
    n = row.shape[1]
    return jnp.sum(jnp.where(iota2((n, n), 0) == iota2((n, n), 1), row, 0.0), axis=1, keepdims=True)


def to_row(column):
    n = column.shape[0]
    return jnp.sum(jnp.where(iota2((n, n), 0) == iota2((n, n), 1), column, 0.0), axis=0, keepdims=True)


def decay_sums(log_row):
    n = log_row.shape[1]
    first, second = iota2((n, n), 0), iota2((n, n), 1)
    g_col = jnp.sum(jnp.where(second <= first, log_row, 0.0), axis=1, keepdims=True)
    return g_col, to_row(g_col)


def softmax_kernel(
    length, base_ref, lens_ref, q_ref, do_ref, kv3, kv2, kv1, kv0,
    dq_ref, part3, part2, part1, own, k_win, v_win, k_t, bias, acc_k, acc_v,
):
    tile, pair = pl.program_id(0), pl.program_id(1)
    first = jnp.logical_and(tile == 0, pair == 0)
    final = jnp.logical_and(tile == pl.num_programs(0) - 1, pair == pl.num_programs(1) - 1)
    rows = q_ref.shape[0]
    reach = bias.shape[0]
    scale = DH ** -0.5

    @pl.when(first)
    def _():
        for slot, kv in enumerate((kv3, kv2, kv1, kv0)):
            here = slice(slot * length, (slot + 1) * length)
            k_win[here, :] = kv[0]
            v_win[here, :] = kv[1]
            k_t[:, here] = kv[0].astype(F32).T.astype(BF16)
        acc_k[...] = jnp.zeros_like(acc_k)
        acc_v[...] = jnp.zeros_like(acc_v)

    @pl.when(pair == 0)
    def _():
        docs = lens_ref.shape[1]
        lens = jnp.where(iota2((docs, docs), 1) <= iota2((docs, docs), 0), lens_ref[...], 0)
        ends = jnp.sum(lens, axis=1, keepdims=True)
        base = base_ref[0] + tile * rows
        t_row = base + iota2((docs, rows), 1)
        start = jnp.max(jnp.where(ends <= t_row, ends, 0), axis=0, keepdims=True)
        s_pos = base - (SUB - 1) * length + iota2((reach, rows), 0)
        t_pos = base + iota2((reach, rows), 1)
        hidden = jnp.where((s_pos <= t_pos) & (s_pos >= start), 0.0, -1e30)
        for head in range(AT_ONCE):
            bias[:, head * rows:(head + 1) * rows] = hidden

    def stacked(ref):
        return jnp.concatenate([ref[:, h * DH:(h + 1) * DH] for h in range(AT_ONCE)], axis=0)

    window = pl.ds(pl.multiple_of(tile * rows, rows), reach)
    q = stacked(q_ref)
    do = stacked(do_ref)
    scores = mm(k_win[window, :], q, NT) * (scale * math.log2(math.e)) + bias[...]
    highest = jnp.max(scores, axis=0, keepdims=True)
    raised = jnp.exp2(scores - highest)
    inverse = 1.0 / jnp.sum(raised, axis=0, keepdims=True)
    grad_probs = mm(v_win[window, :], do, NT)
    delta = jnp.sum(raised * grad_probs, axis=0, keepdims=True) * inverse
    prob = raised * inverse
    dscore = (prob * (grad_probs - delta)).astype(BF16)
    acc_v[window, :] += mm(prob.astype(BF16), do)
    acc_k[window, :] += mm(dscore, q)
    dq = (mm(k_t[:, window], dscore) * scale).T
    for head in range(AT_ONCE):
        dq_ref[:, head * DH:(head + 1) * DH] = dq[head * rows:(head + 1) * rows, :].astype(BF16)

    @pl.when(final)
    def _():
        for slot, out in enumerate((part3, part2, part1, own)):
            here = slice(slot * length, (slot + 1) * length)
            out[:, :DH] = (acc_k[here, :] * scale).astype(out.dtype)
            out[:, DH:] = acc_v[here, :].astype(out.dtype)


def softmax_call(base, lens, q, do, windows):
    length = q.shape[0]
    rows = length // TILES
    whole = lambda *shape: pl.BlockSpec(shape, lambda i, j: (0,) * len(shape))
    per_pair = pl.BlockSpec((rows, AT_ONCE * DH), lambda i, j: (i, j))
    window = SUB * length
    reach = window - length + rows
    pair = jax.ShapeDtypeStruct((length, 2 * DH), BF16)
    return pl.pallas_call(
        functools.partial(softmax_kernel, length),
        out_shape=(
            jax.ShapeDtypeStruct(q.shape, BF16), pair, pair, pair,
            jax.ShapeDtypeStruct((length, 2 * DH), F32),
        ),
        grid=(TILES, GROUP // AT_ONCE),
        in_specs=[
            pl.BlockSpec(memory_space=pltpu.SMEM), whole(1, lens.shape[1]), per_pair, per_pair,
        ] + [whole(2, length, DH)] * SUB,
        out_specs=(per_pair,) + (whole(length, 2 * DH),) * SUB,
        scratch_shapes=[
            pltpu.VMEM((window, DH), BF16), pltpu.VMEM((window, DH), BF16),
            pltpu.VMEM((DH, window), BF16), pltpu.VMEM((reach, AT_ONCE * rows), F32),
            pltpu.VMEM((window, DH), F32), pltpu.VMEM((window, DH), F32),
        ],
        compiler_params=pltpu.CompilerParams(vmem_limit_bytes=VMEM_LIMIT),
        cost_estimate=pl.CostEstimate(
            flops=200 * GROUP * window * length * DH * 4, bytes_accessed=4 * 1024 * 1024,
            transcendentals=GROUP * window * length,
        ),
        name="softmax_backward",
    )(base, lens, q, do, *windows)


def forward_kernel(
    block_ref, q_ref, k_ref, v_ref, gain_ref, log_ref, state_ref, out_ref, gained_ref, scaled_ref, tail_ref
):
    head = pl.program_id(0)
    length = q_ref.shape[0]
    g_col, g_row = decay_sums(log_ref[pl.ds(head, 1), :])
    causal = iota2((length, length), 0) >= iota2((length, length), 1)
    weights = jnp.where(causal, jnp.exp(jnp.minimum(g_col - g_row, 0.0)), 0.0)
    near = (mm(q_ref[...], k_ref[...], NT) * weights).astype(BF16)
    scaled = (q_ref[...].astype(F32) * jnp.exp(g_col)).astype(BF16)
    out = (mm(near, v_ref[...]) + mm(scaled, state_ref[0, 0])) * (1.0 / DH)
    out_ref[...] = out
    gained_ref[...] = (out * gain_ref[...]).astype(BF16)
    scaled_ref[...] = scaled
    tail_ref[...] = jnp.broadcast_to(jnp.exp(g_col[length - 1:, :] - g_col), out.shape)


def per_head_spec(length):
    return pl.BlockSpec((length, DH), lambda h, b: (0, h))


def state_spec():
    return pl.BlockSpec((1, 1, DH, DH), lambda h, b: (0, h, 0, 0))


def log_spec(heads, length):
    return pl.BlockSpec((heads, length), lambda h, b: (0, b[0]))


def forward_call(block, q, k, v, gain, log_decay, state):
    length, heads = q.shape[0], q.shape[1] // DH
    wide = per_head_spec(length)
    like = lambda dtype: jax.ShapeDtypeStruct(q.shape, dtype)
    return pl.pallas_call(
        forward_kernel,
        out_shape=(like(F32), like(BF16), like(BF16), like(F32)),
        grid_spec=pltpu.PrefetchScalarGridSpec(
            num_scalar_prefetch=1, grid=(heads,),
            in_specs=[
                wide, wide, wide, pl.BlockSpec((1, DH), lambda h, b: (0, h)), log_spec(heads, length),
                state_spec(),
            ],
            out_specs=(wide, wide, wide, wide),
        ),
        cost_estimate=pl.CostEstimate(
            flops=heads * length * DH * (4 * length + 2 * DH) * 8, bytes_accessed=4 * 1024 * 1024,
            transcendentals=heads * length * length,
        ),
        name="lightning_forward",
    )(block, q, k, v, gain, log_decay, state)


def pack_kernel(proj_ref, packed_ref):
    packed_ref[:, :, :DH] = proj_ref[0]
    packed_ref[:, :, DH:] = proj_ref[1]


def pack_call(projections, chips):
    rows = projections.shape[1] // chips
    some = chips // 2
    return pl.pallas_call(
        pack_kernel,
        grid=(chips // some,),
        in_specs=[pl.BlockSpec((2, some, rows, DH), lambda i: (0, i, 0, 0))],
        out_specs=pl.BlockSpec((some, rows, 2 * DH), lambda i: (i, 0, 0)),
        out_shape=jax.ShapeDtypeStruct((chips, rows, 2 * DH), BF16),
        cost_estimate=pl.CostEstimate(flops=0, bytes_accessed=4 * 1024 * 1024, transcendentals=0),
        name="pack",
    )(projections.reshape(2, chips, rows, DH))


PARTS = 1


def cotangent_kernel(
    core_ref, dkv_ref, proj_ref, sibling_ref, grad_ref, gain_ref, out_ref,
    gated_ref, carried_ref, stats_ref, squares, cross,
):
    step = pl.program_id(0)
    carried = jnp.zeros(carried_ref.shape, F32)
    for chip in range(dkv_ref.shape[0]):
        carried += mm(dkv_ref[chip], proj_ref[chip], NT)

    @pl.when(step == 0)
    def _():
        squares[...] = jnp.zeros_like(squares)
        cross[...] = jnp.zeros_like(cross)

    @pl.when(step < PARTS)
    def _():
        carried_ref[...] = carried
        cross[...] += jnp.sum(sibling_ref[...].astype(F32) * carried, axis=1, keepdims=True)

    @pl.when(step >= PARTS)
    def _():
        gated = gain_ref[...] * (grad_ref[...].astype(F32) + carried)
        gated_ref[...] = gated
        out = out_ref[...]
        squares[...] += jnp.sum(out * out, axis=1, keepdims=True)
        cross[...] += jnp.sum(gated * out, axis=1, keepdims=True)

    @pl.when(step == pl.num_programs(0) - 1)
    def _():
        rows = iota2(stats_ref.shape[1:], 0)
        stats = jnp.where(
            rows == 0, to_row(squares[...]), jnp.where(rows == 1, to_row(cross[...]), 0.0)
        )
        for copy in range(stats_ref.shape[0]):
            stats_ref[copy] = stats


def cotangent_call(core, dkv, proj, sibling, grad, gain, out):
    length, width = grad.shape
    part = width // PARTS
    whole = lambda *shape: pl.BlockSpec(shape, lambda i, c: (0,) * len(shape))
    early = pl.BlockSpec((length, part), lambda i, c: (0, jnp.minimum(i, PARTS - 1)))
    late = pl.BlockSpec((length, part), lambda i, c: (0, jnp.maximum(i - PARTS, 0)))

    def features(i, c):
        side = jnp.where(i < PARTS, 1 - c[0], c[0])
        return (0, side * PARTS + i % PARTS, 0)

    return pl.pallas_call(
        cotangent_kernel,
        out_shape=(
            jax.ShapeDtypeStruct(grad.shape, F32), jax.ShapeDtypeStruct(grad.shape, F32),
            jax.ShapeDtypeStruct((KV_HEADS, 8, length), F32),
        ),
        grid_spec=pltpu.PrefetchScalarGridSpec(
            num_scalar_prefetch=1, grid=(2 * PARTS,),
            in_specs=[
                whole(*dkv.shape), pl.BlockSpec((dkv.shape[0], part, 2 * DH), features), early, late,
                pl.BlockSpec((1, part), lambda i, c: (0, jnp.maximum(i - PARTS, 0))), late,
            ],
            out_specs=(late, early, whole(KV_HEADS, 8, length)),
            scratch_shapes=[pltpu.VMEM((length, 1), F32), pltpu.VMEM((length, 1), F32)],
        ),
        compiler_params=pltpu.CompilerParams(vmem_limit_bytes=VMEM_LIMIT),
        name="cotangent",
    )(core, dkv, proj, sibling, grad, gain, out)


def dout_kernel(stats_ref, gated_ref, carried_ref, gain_ref, out_ref, scaled_ref, dout_ref, summary_ref):
    stats = stats_ref[0]
    for source in range(1, stats_ref.shape[0]):
        stats += stats_ref[source]
    inverse = 1.0 / jnp.sqrt(stats[0:1, :] * (1.0 / FEATURES) + epsilon)
    factor = stats[1:2, :] * (inverse * inverse * inverse) * (1.0 / FEATURES)
    gated = gated_ref[...] + gain_ref[...] * carried_ref[...]
    low = (gated * to_column(inverse) - out_ref[...] * to_column(factor)).astype(BF16)
    dout_ref[...] = low
    for head in range(summary_ref.shape[0]):
        columns = slice(head * DH, (head + 1) * DH)
        summary_ref[head] = mm(scaled_ref[:, columns], low[:, columns], TN).astype(BF16)


def dout_call(stats, gated, carried, gain, out, scaled):
    return pl.pallas_call(
        dout_kernel,
        out_shape=(
            jax.ShapeDtypeStruct(out.shape, BF16),
            jax.ShapeDtypeStruct((out.shape[1] // DH, DH, DH), BF16),
        ),
        name="dout_summary",
    )(stats, gated, carried, gain, out, scaled)


def near_far_kernel(
    block_ref, q_ref, k_ref, v_ref, dout_ref, log_ref, state_ref, dq_ref, dk_ref, dv_ref
):
    head = pl.program_id(0)
    length = q_ref.shape[0]
    g_col, g_row = decay_sums(log_ref[pl.ds(head, 1), :])
    first, second = iota2((length, length), 0), iota2((length, length), 1)
    gap = g_col - g_row
    weights = jnp.where(first >= second, jnp.exp(jnp.minimum(gap, 0.0)), 0.0)
    turned = jnp.where(second >= first, jnp.exp(jnp.minimum(-gap, 0.0)), 0.0)
    q, k, v, dout = q_ref[...], k_ref[...], v_ref[...], dout_ref[...]
    far = (mm(dout, v, NT) * weights).astype(BF16)
    far_turned = (mm(v, dout, NT) * turned).astype(BF16)
    near_turned = (mm(k, q, NT) * turned).astype(BF16)
    dq = mm(far, k) + jnp.exp(g_col) * mm(dout, state_ref[0, 0], NT)
    dq_ref[...] = (dq * (1.0 / DH)).astype(BF16)
    dk_ref[...] = mm(far_turned, q)
    dv_ref[...] = mm(near_turned, dout)


def near_far_call(block, q, k, v, dout, log_decay, state):
    length, heads = q.shape[0], q.shape[1] // DH
    wide = per_head_spec(length)
    return pl.pallas_call(
        near_far_kernel,
        out_shape=(
            jax.ShapeDtypeStruct(q.shape, BF16), jax.ShapeDtypeStruct(q.shape, F32),
            jax.ShapeDtypeStruct(q.shape, F32),
        ),
        grid_spec=pltpu.PrefetchScalarGridSpec(
            num_scalar_prefetch=1, grid=(heads,),
            in_specs=[wide, wide, wide, wide, log_spec(heads, length), state_spec()],
            out_specs=(wide, wide, wide),
        ),
        cost_estimate=pl.CostEstimate(
            flops=heads * length * DH * (12 * length + 2 * DH) * 8, bytes_accessed=4 * 1024 * 1024,
            transcendentals=2 * heads * length * length,
        ),
        name="near_far",
    )(block, q, k, v, dout, log_decay, state)


def last_kernel(k_ref, v_ref, dk_ref, dv_ref, tail_ref, after_ref, dk_out, dv_out):
    for head in range(after_ref.shape[0]):
        at = slice(head * DH, (head + 1) * DH)
        tail = tail_ref[:, at]
        after = after_ref[head]
        dk = dk_ref[:, at] + tail * mm(v_ref[:, at], after, NT)
        dv = dv_ref[:, at] + tail * mm(k_ref[:, at], after)
        dk_out[:, at] = (dk * (1.0 / DH)).astype(BF16)
        dv_out[:, at] = (dv * (1.0 / DH)).astype(BF16)


def last_call(k, v, dk, dv, tail, after):
    return pl.pallas_call(
        last_kernel,
        out_shape=(jax.ShapeDtypeStruct(k.shape, BF16), jax.ShapeDtypeStruct(k.shape, BF16)),
        name="last",
    )(k, v, dk, dv, tail, after)


ENTER, LEAVE, INNER, CARRY = 0, 16, 32, 96


def state_weights(log_decay, length, device):
    square = QUAD * QUAD
    group, row = device // QUAD % QUAD, device // square
    decays = lax.dynamic_slice_in_dim(log_decay, row, 1, 0)
    gamma = jnp.sum(decays.reshape(-1, length), axis=1)
    block = jnp.arange(gamma.shape[0], dtype=jnp.int32)
    quad = jnp.arange(QUAD, dtype=jnp.int32)
    first = quad * square + group * QUAD
    own = (first[:, None] + quad[None, :]).reshape(-1)
    every = jnp.arange(square, dtype=jnp.int32) * QUAD
    low = jnp.concatenate(
        [jnp.repeat(first - 1, QUAD), own, jnp.repeat(own, QUAD), jnp.repeat(first + QUAD - 1, square)]
    )
    high = jnp.concatenate(
        [own, jnp.repeat(first + QUAD, QUAD), jnp.tile(own.reshape(QUAD, QUAD), (1, QUAD)).reshape(-1),
         jnp.tile(every, QUAD)]
    )
    inside = (block[None, :] > low[:, None]) & (block[None, :] < high[:, None])
    factors = jnp.exp(jnp.sum(jnp.where(inside, gamma[None, :], 0.0), axis=1))
    return jnp.where(high > low, factors, 0.0)


def rise_kernel(weight_ref, blocks_ref, total_ref):
    for row in range(QUAD):
        total = jnp.zeros(blocks_ref.shape[1:], F32)
        for z in range(QUAD):
            at = row * QUAD + z
            total += weight_ref[ENTER + at] * blocks_ref[at].astype(F32)
        total = total.astype(BF16)
        for copy in range(QUAD):
            total_ref[copy, row] = total


def after_kernel(weight_ref, blocks_ref, totals_ref, after_ref):
    square = QUAD * QUAD
    for row in range(QUAD):
        carry = jnp.zeros(blocks_ref.shape[1:], F32)
        for g in range(square):
            carry += weight_ref[CARRY + row * square + g] * totals_ref[g % QUAD, g // QUAD].astype(F32)
        for z in range(QUAD):
            at = row * QUAD + z
            after = weight_ref[LEAVE + at] * carry
            for later in range(z + 1, QUAD):
                after += weight_ref[INNER + at * QUAD + later] * blocks_ref[row * QUAD + later].astype(F32)
            after_ref[at] = after.astype(BF16)


def after_states(summary, weights, beside):
    square = QUAD * QUAD
    rows = lax.axis_size("ctx") // square
    near = [
        [r * square + g * QUAD + z for r in range(rows) for z in range(QUAD)] for g in range(QUAD)
    ]
    far = [[r * square + g * QUAD + z for g in range(QUAD)] for r in range(rows) for z in range(QUAD)]
    smem = pl.BlockSpec(memory_space=pltpu.SMEM)
    vmem = pl.BlockSpec(memory_space=pltpu.VMEM)
    swap = lambda x, groups: lax.all_to_all(x, "ctx", 0, 0, tiled=True, axis_index_groups=groups)
    part = summary.size // square // DH
    blocks = swap(summary.reshape(square, part, DH), near)
    totals = pl.pallas_call(
        rise_kernel, out_shape=jax.ShapeDtypeStruct((QUAD, rows, part, DH), BF16),
        in_specs=[smem, vmem], out_specs=vmem, name="rise",
    )(weights, blocks)
    totals, beside = lax.optimization_barrier((swap(totals, far), beside))
    after = pl.pallas_call(
        after_kernel, out_shape=jax.ShapeDtypeStruct(blocks.shape, BF16),
        in_specs=[smem, vmem, vmem], out_specs=vmem, name="after_states",
    )(weights, blocks, totals)
    return swap(after, near).reshape(summary.shape), beside


def passed_along(block, distance):
    devices = range(lax.axis_size("ctx"))
    route = [(i - distance, i) for i in devices if i - distance in devices]
    return lax.ppermute(block, "ctx", route)


def per_device(
    lin_query, lin_keys, lin_values, lin_grad, norm_gain, log_decay, state_in,
    soft_query, soft_keys, soft_values, soft_grad, projections, doc_lengths,
):
    length = lin_query.shape[0]
    width = lin_query.shape[1]
    device = lax.axis_index("ctx").astype(jnp.int32)
    block = device.reshape(1)

    heads = lax.axis_size("head")
    chips = heads // 2
    same_core = [[2 * chip + core for chip in range(chips)] for core in range(2)]
    sibling = [(i, i ^ 1) for i in range(heads)]
    core = (lax.axis_index("head").astype(jnp.int32) % 2).reshape(1)
    gain = norm_gain.reshape(1, width)

    stacked = jnp.stack([soft_keys, soft_values])
    stacked, early = lax.optimization_barrier((stacked, projections))
    kv2, kv1 = (passed_along(stacked, offset) for offset in (2, 1))
    kv2, packed = lax.optimization_barrier((kv2, pack_call(early, chips)))
    kv3 = passed_along(kv2, 1)
    proj = lax.all_to_all(
        packed, "head", 0, 0, tiled=True, axis_index_groups=same_core
    )
    soft_query = pltpu.with_memory_space_constraint(soft_query, pltpu.HBM)
    soft_grad = pltpu.with_memory_space_constraint(soft_grad, pltpu.HBM)
    soft_dq, part3, part2, part1, own = softmax_call(
        block * length, doc_lengths.reshape(1, -1), soft_query, soft_grad, [kv3, kv2, kv1, stacked]
    )
    beyond = passed_along(part3, -1)
    part1 = passed_along(part1, -1)
    part2 = (part2.astype(F32) + beyond.astype(F32)).astype(BF16)
    part2, lin_query = lax.optimization_barrier((part2, lin_query))
    part2 = passed_along(part2, -2)
    lin_out, gained, scaled, tail = forward_call(
        block, lin_query, lin_keys, lin_values, gain, log_decay, state_in
    )
    dkv = (own + part1.astype(F32) + part2.astype(F32)).astype(BF16)
    copies, lin_out, gained, proj, late_decay = lax.optimization_barrier(
        (jnp.broadcast_to(dkv[None], (chips,) + dkv.shape), lin_out, gained, proj, log_decay)
    )
    weights = state_weights(late_decay, length, device)
    gained = lax.ppermute(gained, "head", sibling)
    soft_dk, soft_dv = dkv[:, :DH], dkv[:, DH:]

    dkv_all = lax.all_to_all(copies, "head", 0, 0, tiled=True, axis_index_groups=same_core)
    gated, carried, stats = cotangent_call(core, dkv_all, proj, gained, lin_grad, gain, lin_out)
    carried = lax.ppermute(carried, "head", sibling)
    stats = lax.all_to_all(stats, "head", 0, 0, tiled=True)
    dout, summary = dout_call(stats, gated, carried, gain, lin_out, scaled)
    beside = near_far_call(block, lin_query, lin_keys, lin_values, dout, log_decay, state_in)
    after, (lin_dq, dk, dv) = after_states(summary, weights, beside)
    lin_dk, lin_dv = last_call(lin_keys, lin_values, dk, dv, tail, after)
    return (lin_dq, lin_dk, lin_dv, soft_dq, soft_dk, soft_dv)


def solution(mesh):
    in_specs = (
        P("ctx", "head"), P("ctx", "head"), P("ctx", "head"), P("ctx", "head"),
        P("head"), P("head", None), P("ctx", "head", None, None),
        P("ctx", "head"), P("ctx", "head"), P("ctx", "head"), P("ctx", "head"),
        P(None, None, "head"), P(),
    )
    out_specs = (P("ctx", "head"),) * 6
    return jax.shard_map(
        per_device, mesh=mesh, in_specs=in_specs, out_specs=out_specs, check_vma=False
    )
```
